32 devices in a mesh: section: 4 (over x, core), ctx: 8 (over z, y).
Axes of the slice: x: 2, y: 2, z: 4, core: 2. Of those that a mesh axis runs over, the one named last changes fastest.
Arguments:
- tokens: bfloat16 [6144, 8192], P(('section', 'ctx')), may hold values from -60 to 60
- norm_gain: float32 [1, 2, 8192], replicated, may hold values from 0.1 to 1.9
- feat_taps: float32 [1, 2, 3, 3, 8192], replicated, may hold values from -3.5 to 3.5
- se_taps: float32 [1, 7, 8192], replicated, may hold values from -2 to 2
- mr_taps: bfloat16 [1, 128, 512], replicated, may hold values from -0.5 to 0.5
Outputs:
- final: bfloat16 [6144, 8192], P(('section', 'ctx'))
The draws below stay inside these ranges and needn't reach their ends.
All inputs are finite; a program needn't handle non-finite values.
Results may differ from the reference program's by a relative error of at most 0.0089.
Values may be sent and summed in bfloat16 or wider, within the bound.
A program may use at most 192 MiB of HBM per device.

```python
import jax
import jax.numpy as jnp
from jax import lax

D = 8192
GROUPS = 512
FEAT = 3
SE_TAPS = 7
MR_TAPS = 128
LAYERS = 1
SEQ = 6144


def draw_tokens(key, part):
    key_base, key_rows, key_cols = jax.random.split(key, 3)
    base = jax.random.truncated_normal(key_base, -6.0, 6.0, (SEQ, D), jnp.float32)
    row_scale = jnp.exp(jax.random.uniform(key_rows, (SEQ, 1), jnp.float32, -1.15, 1.15))
    col_scale = jnp.exp(jax.random.uniform(key_cols, (1, D), jnp.float32, -1.15, 1.15))
    return (base * row_scale * col_scale).astype(jnp.bfloat16)


def noise(own_key, shape, spread, limit, held_as=jnp.bfloat16):
    return jnp.clip(spread * jax.random.normal(own_key, shape, jnp.float32), -limit, limit).astype(held_as)


def setup_inputs(seed: int = 0) -> dict:
    keys = jax.random.split(jax.random.key(seed), 6)
    tokens = draw_tokens(jax.random.fold_in(keys[5], 71), 0)
    norm_gain = jnp.clip(1.0 + 0.18 * jax.random.normal(keys[1], (LAYERS, 2, D), jnp.float32), 0.1, 1.9)
    feat_taps = noise(keys[2], (LAYERS, 2, 3, FEAT, D), FEAT ** -0.5, 3.5, jnp.float32)
    se_taps = noise(keys[3], (LAYERS, SE_TAPS, D), SE_TAPS ** -0.5, 2.0, jnp.float32)
    mr_taps = noise(keys[4], (LAYERS, MR_TAPS, GROUPS), MR_TAPS ** -0.5, 0.5)
    return {"tokens": tokens, "norm_gain": norm_gain, "feat_taps": feat_taps, "se_taps": se_taps, "mr_taps": mr_taps}


def normalize(hidden, gain):
    values = hidden.astype(jnp.float32)
    mean_square = lax.optimization_barrier(jnp.mean(values * values, axis=-1, keepdims=True))
    return values * lax.rsqrt(mean_square + 1e-06) * gain

def delay(values, lag_rows):
    return jnp.pad(values, ((lag_rows, 0), (0, 0)))[:values.shape[0]]

def short_filter(product, filter_taps):
    values = product.astype(jnp.float32)
    summed = filter_taps[0] * values
    for i in range(1, filter_taps.shape[0]):
        summed = summed + filter_taps[i] * delay(values, i)
    return summed

def long_filter(product, filter_taps):
    values = product.astype(jnp.float32)
    row_total = values.shape[0]
    tap_count = filter_taps.shape[0]
    factor = values.shape[1] // filter_taps.shape[1]
    full_taps = jnp.repeat(filter_taps.astype(jnp.float32), factor, axis=1)
    padded = jnp.pad(values, ((tap_count - 1, 0), (0, 0)))

    def accumulate(i, summed):
        window_rows = lax.dynamic_slice_in_dim(padded, tap_count - 1 - i, row_total, 0)
        tap_row = lax.dynamic_index_in_dim(full_taps, i, 0, keepdims=False)
        return summed + tap_row * window_rows
    return lax.fori_loop(0, tap_count, accumulate, jnp.zeros(values.shape, jnp.float32))

def apply_operator(hidden, gain, feature_taps, filter_fn):
    scaled = normalize(hidden, gain)
    streams = []
    for j in range(3):
        summed = feature_taps[j, 0] * scaled
        for i in range(1, feature_taps.shape[1]):
            summed = summed + feature_taps[j, i] * delay(scaled, i)
        streams.append(summed)
    product = (streams[1] * streams[2]).astype(jnp.bfloat16)
    filtered = filter_fn(product)
    return (hidden.astype(jnp.float32) + streams[0] * filtered).astype(jnp.bfloat16)

def reference(tokens, norm_gain, feat_taps, se_taps, mr_taps):
    hidden = tokens
    for layer in range(LAYERS):
        short_taps = se_taps[layer]
        long_taps = mr_taps[layer]
        hidden = apply_operator(hidden, norm_gain[layer, 0], feat_taps[layer, 0], lambda p: short_filter(p, short_taps))
        hidden = apply_operator(hidden, norm_gain[layer, 1], feat_taps[layer, 1], lambda p: long_filter(p, long_taps))
    return hidden
```

```python
import functools

import jax
import jax.numpy as jnp
from jax import lax
from jax.experimental import pallas as pl
from jax.experimental.pallas import tpu as pltpu
from jax.sharding import PartitionSpec as P

F32 = jnp.float32
BF16 = jnp.bfloat16
LANES = 128
CHUNKS = 16
EARLY = 4
STEP = 4
LEAD = 16
MESH = pl.DeviceIdType.MESH


def lanes_of(c, width=LANES):
    return pl.ds(pl.multiple_of(c * width, width), width)


def row_scale(total, channels):
    mean = jnp.sum(total, axis=-1, keepdims=True) * (1.0 / channels)
    return jnp.broadcast_to(lax.rsqrt(mean + 1e-06), total.shape)


def square_sums(read, rows, blocks):
    def add(c, total):
        v = read(c).astype(F32)
        return total + v * v

    return lax.fori_loop(0, blocks, add, jnp.zeros((rows, LANES), F32))


def stream(z_ref, taps, first, rows):
    total = taps[0] * z_ref[8 + first : 8 + first + rows]
    for i in range(1, len(taps)):
        total = total + taps[i] * z_ref[8 + first - i : 8 + first - i + rows]
    return total


def feat_rows(feat_ref, o, gain, cs):
    streams, feat = feat_ref.shape[1:3]
    return [[feat_ref[0, j, i, o : o + 1, cs] * gain for i in range(feat)] for j in range(streams)]


def pieces(rows, most=48):
    return [(first, min(most, rows - first)) for first in range(0, rows, most)]


def short_block(c, read, rows, gain_ref, feat_ref, taps_ref, z_ref, w_ref, s_ref, h_ref, start, hs):
    cs = lanes_of(c)
    gain = gain_ref[0, 0:1, cs]
    taps = feat_rows(feat_ref, 0, gain, cs)
    short = [taps_ref[i, 0:1, cs] for i in range(taps_ref.shape[0])]
    z_ref[8 : 8 + rows] = read(c).astype(F32) * s_ref[:rows]
    for first, count in pieces(rows):
        u1 = stream(z_ref, taps[1], first, count)
        u2 = stream(z_ref, taps[2], first, count)
        w_ref[8 + first : 8 + first + count] = (u1 * u2).astype(BF16).astype(F32)
    for first, count in pieces(rows):
        f = stream(w_ref, short, first, count)
        u0 = stream(z_ref, taps[0], first, count)
        h_ref[start + first : start + first + count, hs] = u0 * f
    h = (h_ref[start : start + rows, hs] + read(c).astype(F32)).astype(BF16).astype(F32)
    h_ref[start : start + rows, hs] = h
    return h


def same_place(rows):
    return (lax.broadcasted_iota(jnp.int32, (rows, LANES), 0)
            == lax.broadcasted_iota(jnp.int32, (rows, LANES), 1))


def pack_rows(values_ref, start, rows, pack_ref):
    for r, (first, count) in enumerate(pieces(rows, LANES)):
        values = values_ref[start + first : start + first + count]
        pack_ref[r : r + 1] = jnp.sum(jnp.where(same_place(count), values, 0.0), axis=0, keepdims=True)


def unpack_rows(pack_ref, rows, values_ref):
    for r, (first, count) in enumerate(pieces(rows, LANES)):
        values = jnp.broadcast_to(pack_ref[r : r + 1], (count, LANES))
        column = jnp.sum(jnp.where(same_place(count), values, 0.0), axis=1, keepdims=True)
        values_ref[first : first + count] = jnp.broadcast_to(column, (count, LANES))


def kernel(axes, x_hbm, gain_hbm, feat_hbm, taps_hbm, mr_hbm, out_ref,
           x_ref, gain_ref, feat_ref, taps_ref, mr_ref,
           lead_ref, win_ref, h_ref, u_ref, table_ref, base_ref, rhs_ref, scale_ref, z_ref, w_ref,
           s_ref, sum_ref, halo_ref, told_ref, give_ref, got_ref, local_sems, lead_sems, send_sems, recv_sems):
    rows, channels = x_ref.shape
    tap_count, group_count = mr_ref.shape[1:]
    per_group = channels // group_count
    groups = LANES // per_group
    half = rows // 2
    blocks = channels // LANES
    part = channels // CHUNKS
    here = blocks // CHUNKS
    tail = tap_count + LEAD
    first_tail = rows - tail
    first_sent = rows - tap_count
    outer, inner = axes
    inner_size = lax.axis_size(inner)
    count = lax.axis_size(outer) * inner_size
    me = lax.axis_index(outer) * inner_size + lax.axis_index(inner)
    behind, ahead = me - 1, me + 1
    has_behind, has_ahead = me > 0, me < count - 1

    def place(index):
        return (index // inner_size, index % inner_size)

    barrier = pltpu.get_barrier_semaphore()

    @pl.when(has_behind)
    def _():
        pl.semaphore_signal(barrier, inc=1, device_id=place(behind), device_id_type=MESH)

    loads = [pltpu.make_async_copy(src, dst, local_sems.at[i]) for i, (src, dst) in enumerate(
        [(x_hbm, x_ref), (gain_hbm, gain_ref), (feat_hbm, feat_ref), (taps_hbm, taps_ref), (mr_hbm, mr_ref)])]
    for load in loads:
        load.start()

    def to_ahead(src, dst, send_sem, recv_sem):
        return pltpu.make_async_remote_copy(
            src_ref=src, dst_ref=dst, send_sem=send_sem, recv_sem=recv_sem,
            device_id=place(ahead), device_id_type=MESH)

    def lead_copy():
        return to_ahead(x_hbm.at[pl.ds(rows - LEAD, LEAD)], lead_ref, lead_sems.at[0], lead_sems.at[1])

    def tell_copy(o):
        return to_ahead(give_ref.at[o], got_ref.at[o], lead_sems.at[2 + 2 * o], lead_sems.at[3 + 2 * o])

    def early_copy(k):
        cs = lanes_of(k, part)
        return to_ahead(x_hbm.at[pl.ds(first_tail, tap_count), cs], win_ref.at[pl.ds(0, tap_count), cs],
                        send_sems.at[k], recv_sems.at[k])

    def part_copy(k):
        cs = lanes_of(k, part)
        return to_ahead(win_ref.at[pl.ds(rows, tap_count), cs], win_ref.at[pl.ds(0, tap_count), cs],
                        send_sems.at[k], recv_sems.at[k])

    @pl.when(has_ahead)
    def _():
        pl.semaphore_wait(barrier, 1)
        lead_copy().start()

        @pl.loop(0, EARLY)
        def _(k):
            early_copy(k).start()

    z_ref[...] = jnp.zeros_like(z_ref)
    w_ref[...] = jnp.zeros_like(w_ref)
    give_ref[...] = jnp.zeros_like(give_ref)
    share = (gain_ref, feat_ref, taps_ref, z_ref, w_ref, s_ref)
    early_blocks = EARLY * here

    def mr_product(taps, first, size):
        return (stream(z_ref, taps[1], first, size) * stream(z_ref, taps[2], first, size)).astype(BF16)

    def mr_taps_of(cs):
        return feat_rows(feat_ref, 1, gain_ref[0, 1:2, cs], cs)

    loads[0].wait()
    read_tail = lambda c: x_ref[first_tail:, lanes_of(c)]
    s_ref[:tail] = row_scale(square_sums(read_tail, tail, blocks), channels)
    pack_rows(s_ref, 0, tail, give_ref.at[0])

    @pl.when(has_ahead)
    def _():
        tell_copy(0).start()

    for load in loads[1:]:
        load.wait()
    sum_ref[:tail] = jnp.zeros((tail, LANES), F32)
    start_tail = LEAD + first_tail

    @pl.loop(0, blocks)
    def _(c):
        h = short_block(c, read_tail, tail, *share, h_ref, start_tail, lanes_of(c))
        sum_ref[:tail] += h * h

    scale_ref[start_tail : start_tail + tail] = row_scale(sum_ref[:tail], channels)
    pack_rows(scale_ref, start_tail, tail, give_ref.at[1])

    @pl.when(has_ahead)
    def _():
        tell_copy(1).start()

    @pl.loop(EARLY, CHUNKS)
    def _(k):
        @pl.loop(0, here)
        def _(b):
            cs = lanes_of(k * here + b)
            taps = mr_taps_of(cs)
            n = tap_count + 8
            top = LEAD + first_sent - 8
            z_ref[0:n] = h_ref[top : top + n, cs] * scale_ref[top : top + n]
            for first, size in pieces(tap_count):
                win_ref[rows + first : rows + first + size, cs] = mr_product(taps, first, size)

        @pl.when(has_ahead)
        def _():
            part_copy(k).start()

    at_tap = lax.broadcasted_iota(jnp.int32, (tap_count, tap_count), 0)
    at_lag = lax.broadcasted_iota(jnp.int32, (tap_count, tap_count), 1)
    flip = jnp.where((at_tap + at_lag == tap_count) | (at_tap + at_lag == 0), 1.0, 0.0).astype(BF16)
    past = (lax.broadcasted_iota(jnp.int32, (half, tap_count), 1)
            > lax.broadcasted_iota(jnp.int32, (half, tap_count), 0))
    base_ref[...] = lax.dot_general(mr_ref[0], flip, (((0,), (0,)), ((), ())),
                                    preferred_element_type=F32)
    rhs_ref[...] = jnp.zeros_like(rhs_ref)

    @pl.when(has_behind)
    def _():
        lead_copy().wait_recv()

    @pl.when(jnp.logical_not(has_behind))
    def _():
        lead_ref[...] = jnp.zeros_like(lead_ref)
        win_ref[:tap_count] = jnp.zeros((tap_count, channels), BF16)

    head = LEAD + first_sent
    z_ref[0:8] = jnp.zeros((8, LANES), F32)
    read_head = lambda c: jnp.concatenate(
        [lead_ref[:, lanes_of(c)], x_ref[:first_sent, lanes_of(c)]], axis=0)
    s_ref[:head] = row_scale(square_sums(read_head, head, blocks), channels)
    sum_ref[:head] = jnp.zeros((head, LANES), F32)

    @pl.loop(0, blocks)
    def _(c):
        h = short_block(c, read_head, head, *share, h_ref, 0, lanes_of(c))
        sum_ref[:head] += h * h

    scale_ref[:head] = row_scale(sum_ref[:head], channels)

    @pl.loop(0, blocks)
    def _(c):
        cs = lanes_of(c)
        taps = mr_taps_of(cs)
        z_ref[0 : rows + 8] = h_ref[LEAD - 8 :, cs] * scale_ref[LEAD - 8 :]

        def put(low, high):
            for first, size in pieces(high - low):
                first += low
                win_ref[tap_count + first : tap_count + first + size, cs] = mr_product(taps, first, size)

        put(0, first_sent)

        @pl.when(c < early_blocks)
        def _():
            put(first_sent, rows)

        for first, size in pieces(rows):
            u_ref[first : first + size, cs] = stream(z_ref, taps[0], first, size)

    @pl.loop(0, blocks)
    def _(c):
        lags = base_ref[pl.ds(pl.multiple_of(c * groups, groups), groups), :]
        for g in range(groups):
            row = jnp.broadcast_to(lags[g : g + 1], (half, tap_count))
            turned = pltpu.roll(row, 0, 1, stride=1, stride_axis=0)
            gs = slice(g * half, (g + 1) * half)
            table_ref[c, gs, :tap_count] = jnp.where(past, turned, 0.0).astype(BF16)
            table_ref[c, gs, tap_count:] = jnp.where(past, 0.0, turned).astype(BF16)

    lane_group = lax.broadcasted_iota(jnp.int32, (half, LANES), 1) // per_group
    reach = half + tap_count

    @pl.when(has_behind)
    def _():
        tell_copy(0).wait_recv()
        unpack_rows(got_ref.at[0], tail, s_ref)
        tell_copy(1).wait_recv()
        unpack_rows(got_ref.at[1], tail, told_ref)

    @pl.loop(0, CHUNKS)
    def _(k):
        @pl.when(has_behind)
        def _():
            part_copy(k).wait_recv()

        @pl.when(has_behind & (k < EARLY))
        def _():
            @pl.loop(0, here)
            def _(b):
                c = k * here + b
                cs = lanes_of(c)
                read_halo = lambda _: jnp.concatenate([win_ref[:tap_count, cs], lead_ref[:, cs]], axis=0)
                short_block(c, read_halo, tail, *share, halo_ref, 0, slice(None))
                taps = mr_taps_of(cs)
                z_ref[0:tail] = halo_ref[...] * told_ref[...]
                for first, size in pieces(tap_count):
                    win_ref[first : first + size, cs] = mr_product(taps, tail - tap_count - 8 + first, size)

        @pl.loop(0, here, step=STEP)
        def _(b):
          for slot in range(STEP):
            c = k * here + b + slot
            cs = lanes_of(c)
            rhs_ref[slot, :reach, :LANES] = win_ref[:reach, cs]
            rhs_ref[slot, :reach, LANES:] = win_ref[half : half + reach, cs]
            product = jnp.dot(table_ref[c], rhs_ref[slot], preferred_element_type=F32)
            for side in range(2):
                ls = slice(side * LANES, (side + 1) * LANES)
                f = product[0:half, ls]
                for g in range(1, groups):
                    f = jnp.where(lane_group == g, product[g * half : (g + 1) * half, ls], f)
                rs = slice(side * half, (side + 1) * half)
                hs = slice(LEAD + side * half, LEAD + (side + 1) * half)
                out_ref[rs, cs] = (h_ref[hs, cs] + u_ref[rs, cs] * f).astype(BF16)

    @pl.when(has_ahead)
    def _():
        lead_copy().wait_send()
        tell_copy(0).wait_send()
        tell_copy(1).wait_send()

        @pl.loop(0, CHUNKS)
        def _(k):
            part_copy(k).wait_send()


def on_device(axes, tokens, norm_gain, feat_taps, se_taps, mr_taps):
    rows, channels = tokens.shape
    tap_count, group_count = mr_taps.shape[1:]
    groups = LANES * group_count // channels
    blocks = channels // LANES
    spread = 2 * tap_count
    operands = (tokens, norm_gain, feat_taps.transpose(0, 2, 3, 1, 4), se_taps.transpose(1, 0, 2), mr_taps)
    return pl.pallas_call(
        functools.partial(kernel, axes),
        out_shape=jax.ShapeDtypeStruct((rows, channels), BF16),
        in_specs=[pl.BlockSpec(memory_space=pltpu.HBM)] * 5,
        out_specs=pl.BlockSpec(memory_space=pltpu.VMEM),
        scratch_shapes=[pltpu.VMEM(a.shape, a.dtype) for a in operands] + [
            pltpu.VMEM((LEAD, channels), BF16),
            pltpu.VMEM((tap_count + rows, channels), BF16),
            pltpu.VMEM((LEAD + rows, channels), F32),
            pltpu.VMEM((rows, channels), F32),
            pltpu.VMEM((blocks, groups * rows // 2, spread), BF16),
            pltpu.VMEM((group_count, tap_count), F32),
            pltpu.VMEM((STEP, spread, 2 * LANES), BF16),
            pltpu.VMEM((LEAD + rows, LANES), F32),
            pltpu.VMEM((LEAD + rows, LANES), F32),
            pltpu.VMEM((LEAD + rows, LANES), F32),
            pltpu.VMEM((LEAD + rows, LANES), F32),
            pltpu.VMEM((LEAD + rows, LANES), F32),
            pltpu.VMEM((tap_count + LEAD, LANES), F32),
            pltpu.VMEM((tap_count + LEAD, LANES), F32),
            pltpu.VMEM((2, 8, LANES), F32),
            pltpu.VMEM((2, 8, LANES), F32),
            pltpu.SemaphoreType.DMA((5,)),
            pltpu.SemaphoreType.DMA((6,)),
            pltpu.SemaphoreType.DMA((CHUNKS,)),
            pltpu.SemaphoreType.DMA((CHUNKS,)),
        ],
        compiler_params=pltpu.CompilerParams(
            collective_id=0, has_side_effects=True, vmem_limit_bytes=67043328),
        name="pair",
    )(*operands)


def solution(mesh):
    axes = tuple(mesh.axis_names)
    placed = (P(axes, None), P(), P(), P(), P())
    return jax.shard_map(
        functools.partial(on_device, axes),
        mesh=mesh,
        in_specs=placed,
        out_specs=P(axes, None),
        check_vma=False,
    )
```

```python
import functools

import jax
import jax.numpy as jnp
from jax import lax
from jax.experimental import pallas as pl
from jax.experimental.pallas import tpu as pltpu
from jax.sharding import PartitionSpec as P

F32 = jnp.float32
BF16 = jnp.bfloat16
LANES = 128
CHUNKS = 16
EARLY = 4
STEP = 4
LEAD = 16
MESH = pl.DeviceIdType.MESH


def lanes_of(c, width=LANES):
    return pl.ds(pl.multiple_of(c * width, width), width)


def row_scale(total, channels):
    mean = jnp.sum(total, axis=-1, keepdims=True) * (1.0 / channels)
    return jnp.broadcast_to(lax.rsqrt(mean + 1e-06), total.shape)


def square_sums(read, rows, blocks):
    def add(c, total):
        v = read(c).astype(F32)
        return total + v * v

    return lax.fori_loop(0, blocks, add, jnp.zeros((rows, LANES), F32))


def stream(z_ref, taps, first, rows):
    total = taps[0] * z_ref[8 + first : 8 + first + rows]
    for i in range(1, len(taps)):
        total = total + taps[i] * z_ref[8 + first - i : 8 + first - i + rows]
    return total


def feat_rows(feat_ref, o, gain, cs):
    streams, feat = feat_ref.shape[1:3]
    return [[feat_ref[0, j, i, o : o + 1, cs] * gain for i in range(feat)] for j in range(streams)]


def pieces(rows, most=48):
    return [(first, min(most, rows - first)) for first in range(0, rows, most)]


def short_block(c, read, rows, gain_ref, feat_ref, taps_ref, z_ref, w_ref, s_ref, h_ref, start, hs):
    cs = lanes_of(c)
    gain = gain_ref[0, 0:1, cs]
    taps = feat_rows(feat_ref, 0, gain, cs)
    short = [taps_ref[i, 0:1, cs] for i in range(taps_ref.shape[0])]
    z_ref[8 : 8 + rows] = read(c).astype(F32) * s_ref[:rows]
    for first, count in pieces(rows):
        u1 = stream(z_ref, taps[1], first, count)
        u2 = stream(z_ref, taps[2], first, count)
        w_ref[8 + first : 8 + first + count] = (u1 * u2).astype(BF16).astype(F32)
    for first, count in pieces(rows):
        f = stream(w_ref, short, first, count)
        u0 = stream(z_ref, taps[0], first, count)
        h_ref[start + first : start + first + count, hs] = u0 * f
    h = (h_ref[start : start + rows, hs] + read(c).astype(F32)).astype(BF16).astype(F32)
    h_ref[start : start + rows, hs] = h
    return h


def same_place(rows):
    return (lax.broadcasted_iota(jnp.int32, (rows, LANES), 0)
            == lax.broadcasted_iota(jnp.int32, (rows, LANES), 1))


def pack_rows(values_ref, start, rows, pack_ref):
    for r, (first, count) in enumerate(pieces(rows, LANES)):
        values = values_ref[start + first : start + first + count]
        pack_ref[r : r + 1] = jnp.sum(jnp.where(same_place(count), values, 0.0), axis=0, keepdims=True)


def unpack_rows(pack_ref, rows, values_ref):
    for r, (first, count) in enumerate(pieces(rows, LANES)):
        values = jnp.broadcast_to(pack_ref[r : r + 1], (count, LANES))
        column = jnp.sum(jnp.where(same_place(count), values, 0.0), axis=1, keepdims=True)
        values_ref[first : first + count] = jnp.broadcast_to(column, (count, LANES))


def kernel(axes, x_hbm, gain_hbm, feat_hbm, taps_hbm, mr_hbm, out_ref,
           x_ref, gain_ref, feat_ref, taps_ref, mr_ref,
           lead_ref, win_ref, h_ref, u_ref, table_ref, base_ref, rhs_ref, scale_ref, z_ref, w_ref,
           s_ref, sum_ref, halo_ref, told_ref, give_ref, got_ref, local_sems, lead_sems, send_sems, recv_sems):
    rows, channels = x_ref.shape
    tap_count, group_count = mr_ref.shape[1:]
    per_group = channels // group_count
    groups = LANES // per_group
    half = rows // 2
    blocks = channels // LANES
    part = channels // CHUNKS
    here = blocks // CHUNKS
    tail = tap_count + LEAD
    first_tail = rows - tail
    first_sent = rows - tap_count
    outer, inner = axes
    inner_size = lax.axis_size(inner)
    count = lax.axis_size(outer) * inner_size
    me = lax.axis_index(outer) * inner_size + lax.axis_index(inner)
    behind, ahead = me - 1, me + 1
    has_behind, has_ahead = me > 0, me < count - 1

    def place(index):
        return (index // inner_size, index % inner_size)

    barrier = pltpu.get_barrier_semaphore()

    @pl.when(has_behind)
    def _():
        pl.semaphore_signal(barrier, inc=1, device_id=place(behind), device_id_type=MESH)

    loads = [pltpu.make_async_copy(src, dst, local_sems.at[i]) for i, (src, dst) in enumerate(
        [(x_hbm, x_ref), (gain_hbm, gain_ref), (feat_hbm, feat_ref), (taps_hbm, taps_ref), (mr_hbm, mr_ref)])]
    for load in loads:
        load.start()

    def to_ahead(src, dst, send_sem, recv_sem):
        return pltpu.make_async_remote_copy(
            src_ref=src, dst_ref=dst, send_sem=send_sem, recv_sem=recv_sem,
            device_id=place(ahead), device_id_type=MESH)

    def lead_copy():
        return to_ahead(x_hbm.at[pl.ds(rows - LEAD, LEAD)], lead_ref, lead_sems.at[0], lead_sems.at[1])

    def tell_copy(o):
        return to_ahead(give_ref.at[o], got_ref.at[o], lead_sems.at[2 + 2 * o], lead_sems.at[3 + 2 * o])

    def early_copy(k):
        cs = lanes_of(k, part)
        return to_ahead(x_hbm.at[pl.ds(first_tail, tap_count), cs], win_ref.at[pl.ds(0, tap_count), cs],
                        send_sems.at[k], recv_sems.at[k])

    def part_copy(k):
        cs = lanes_of(k, part)
        return to_ahead(win_ref.at[pl.ds(rows, tap_count), cs], win_ref.at[pl.ds(0, tap_count), cs],
                        send_sems.at[k], recv_sems.at[k])

    @pl.when(has_ahead)
    def _():
        pl.semaphore_wait(barrier, 1)
        lead_copy().start()

        @pl.loop(0, EARLY)
        def _(k):
            early_copy(k).start()

    z_ref[...] = jnp.zeros_like(z_ref)
    w_ref[...] = jnp.zeros_like(w_ref)
    give_ref[...] = jnp.zeros_like(give_ref)
    share = (gain_ref, feat_ref, taps_ref, z_ref, w_ref, s_ref)
    early_blocks = EARLY * here

    def mr_product(taps, first, size):
        return (stream(z_ref, taps[1], first, size) * stream(z_ref, taps[2], first, size)).astype(BF16)

    def mr_taps_of(cs):
        return feat_rows(feat_ref, 1, gain_ref[0, 1:2, cs], cs)

    loads[0].wait()
    read_tail = lambda c: x_ref[first_tail:, lanes_of(c)]
    s_ref[:tail] = row_scale(square_sums(read_tail, tail, blocks), channels)
    pack_rows(s_ref, 0, tail, give_ref.at[0])

    @pl.when(has_ahead)
    def _():
        tell_copy(0).start()

    for load in loads[1:]:
        load.wait()
    sum_ref[:tail] = jnp.zeros((tail, LANES), F32)
    start_tail = LEAD + first_tail

    @pl.loop(0, blocks)
    def _(c):
        h = short_block(c, read_tail, tail, *share, h_ref, start_tail, lanes_of(c))
        sum_ref[:tail] += h * h

    scale_ref[start_tail : start_tail + tail] = row_scale(sum_ref[:tail], channels)
    pack_rows(scale_ref, start_tail, tail, give_ref.at[1])

    @pl.when(has_ahead)
    def _():
        tell_copy(1).start()

    @pl.loop(EARLY, CHUNKS)
    def _(k):
        @pl.loop(0, here)
        def _(b):
            cs = lanes_of(k * here + b)
            taps = mr_taps_of(cs)
            n = tap_count + 8
            top = LEAD + first_sent - 8
            z_ref[0:n] = h_ref[top : top + n, cs] * scale_ref[top : top + n]
            for first, size in pieces(tap_count):
                win_ref[rows + first : rows + first + size, cs] = mr_product(taps, first, size)

        @pl.when(has_ahead)
        def _():
            part_copy(k).start()

    at_tap = lax.broadcasted_iota(jnp.int32, (tap_count, tap_count), 0)
    at_lag = lax.broadcasted_iota(jnp.int32, (tap_count, tap_count), 1)
    flip = jnp.where((at_tap + at_lag == tap_count) | (at_tap + at_lag == 0), 1.0, 0.0).astype(BF16)
    past = (lax.broadcasted_iota(jnp.int32, (half, tap_count), 1)
            > lax.broadcasted_iota(jnp.int32, (half, tap_count), 0))
    base_ref[...] = lax.dot_general(mr_ref[0], flip, (((0,), (0,)), ((), ())),
                                    preferred_element_type=F32)
    rhs_ref[...] = jnp.zeros_like(rhs_ref)

    @pl.when(has_behind)
    def _():
        lead_copy().wait_recv()

    @pl.when(jnp.logical_not(has_behind))
    def _():
        lead_ref[...] = jnp.zeros_like(lead_ref)
        win_ref[:tap_count] = jnp.zeros((tap_count, channels), BF16)

    head = LEAD + first_sent
    z_ref[0:8] = jnp.zeros((8, LANES), F32)
    read_head = lambda c: jnp.concatenate(
        [lead_ref[:, lanes_of(c)], x_ref[:first_sent, lanes_of(c)]], axis=0)
    s_ref[:head] = row_scale(square_sums(read_head, head, blocks), channels)
    sum_ref[:head] = jnp.zeros((head, LANES), F32)

    @pl.loop(0, blocks)
    def _(c):
        h = short_block(c, read_head, head, *share, h_ref, 0, lanes_of(c))
        sum_ref[:head] += h * h

    scale_ref[:head] = row_scale(sum_ref[:head], channels)

    @pl.loop(0, blocks)
    def _(c):
        cs = lanes_of(c)
        taps = mr_taps_of(cs)
        z_ref[0 : rows + 8] = h_ref[LEAD - 8 :, cs] * scale_ref[LEAD - 8 :]

        def put(low, high):
            for first, size in pieces(high - low):
                first += low
                win_ref[tap_count + first : tap_count + first + size, cs] = mr_product(taps, first, size)

        put(0, first_sent)

        @pl.when(c < early_blocks)
        def _():
            put(first_sent, rows)

        for first, size in pieces(rows):
            u_ref[first : first + size, cs] = stream(z_ref, taps[0], first, size)

    @pl.loop(0, blocks)
    def _(c):
        lags = base_ref[pl.ds(pl.multiple_of(c * groups, groups), groups), :]
        for g in range(groups):
            row = jnp.broadcast_to(lags[g : g + 1], (half, tap_count))
            turned = pltpu.roll(row, 0, 1, stride=1, stride_axis=0)
            gs = slice(g * half, (g + 1) * half)
            table_ref[c, gs, :tap_count] = jnp.where(past, turned, 0.0).astype(BF16)
            table_ref[c, gs, tap_count:] = jnp.where(past, 0.0, turned).astype(BF16)

    lane_group = lax.broadcasted_iota(jnp.int32, (half, LANES), 1) // per_group
    reach = half + tap_count

    @pl.when(has_behind)
    def _():
        tell_copy(0).wait_recv()
        unpack_rows(got_ref.at[0], tail, s_ref)
        tell_copy(1).wait_recv()
        unpack_rows(got_ref.at[1], tail, told_ref)

    @pl.loop(0, CHUNKS)
    def _(k):
        @pl.when(has_behind)
        def _():
            part_copy(k).wait_recv()

        @pl.when(has_behind & (k < EARLY))
        def _():
            @pl.loop(0, here)
            def _(b):
                c = k * here + b
                cs = lanes_of(c)
                read_halo = lambda _: jnp.concatenate([win_ref[:tap_count, cs], lead_ref[:, cs]], axis=0)
                short_block(c, read_halo, tail, *share, halo_ref, 0, slice(None))
                taps = mr_taps_of(cs)
                z_ref[0:tail] = halo_ref[...] * told_ref[...]
                for first, size in pieces(tap_count):
                    win_ref[first : first + size, cs] = mr_product(taps, tail - tap_count - 8 + first, size)

        @pl.loop(0, here, step=STEP)
        def _(b):
          for slot in range(STEP):
            c = k * here + b + slot
            cs = lanes_of(c)
            rhs_ref[slot, :reach, :LANES] = win_ref[:reach, cs]
            rhs_ref[slot, :reach, LANES:] = win_ref[half : half + reach, cs]
            product = jnp.dot(table_ref[c], rhs_ref[slot], preferred_element_type=F32)
            for side in range(2):
                ls = slice(side * LANES, (side + 1) * LANES)
                f = product[0:half, ls]
                for g in range(1, groups):
                    f = jnp.where(lane_group == g, product[g * half : (g + 1) * half, ls], f)
                rs = slice(side * half, (side + 1) * half)
                hs = slice(LEAD + side * half, LEAD + (side + 1) * half)
                out_ref[rs, cs] = (h_ref[hs, cs] + u_ref[rs, cs] * f).astype(BF16)

    @pl.when(has_ahead)
    def _():
        lead_copy().wait_send()
        tell_copy(0).wait_send()
        tell_copy(1).wait_send()

        @pl.loop(0, CHUNKS)
        def _(k):
            part_copy(k).wait_send()


def on_device(axes, tokens, norm_gain, feat_taps, se_taps, mr_taps):
    rows, channels = tokens.shape
    tap_count, group_count = mr_taps.shape[1:]
    groups = LANES * group_count // channels
    blocks = channels // LANES
    spread = 2 * tap_count
    operands = (tokens, norm_gain, feat_taps.transpose(0, 2, 3, 1, 4), se_taps.transpose(1, 0, 2), mr_taps)
    return pl.pallas_call(
        functools.partial(kernel, axes),
        out_shape=pltpu.VMEM((rows, channels), BF16),
        in_specs=[pl.BlockSpec(memory_space=pltpu.HBM)] * 5,
        out_specs=pl.BlockSpec(memory_space=pltpu.VMEM),
        scratch_shapes=[pltpu.VMEM(a.shape, a.dtype) for a in operands] + [
            pltpu.VMEM((LEAD, channels), BF16),
            pltpu.VMEM((tap_count + rows, channels), BF16),
            pltpu.VMEM((LEAD + rows, channels), F32),
            pltpu.VMEM((rows, channels), F32),
            pltpu.VMEM((blocks, groups * rows // 2, spread), BF16),
            pltpu.VMEM((group_count, tap_count), F32),
            pltpu.VMEM((STEP, spread, 2 * LANES), BF16),
            pltpu.VMEM((LEAD + rows, LANES), F32),
            pltpu.VMEM((LEAD + rows, LANES), F32),
            pltpu.VMEM((LEAD + rows, LANES), F32),
            pltpu.VMEM((LEAD + rows, LANES), F32),
            pltpu.VMEM((LEAD + rows, LANES), F32),
            pltpu.VMEM((tap_count + LEAD, LANES), F32),
            pltpu.VMEM((tap_count + LEAD, LANES), F32),
            pltpu.VMEM((2, 8, LANES), F32),
            pltpu.VMEM((2, 8, LANES), F32),
            pltpu.SemaphoreType.DMA((5,)),
            pltpu.SemaphoreType.DMA((6,)),
            pltpu.SemaphoreType.DMA((CHUNKS,)),
            pltpu.SemaphoreType.DMA((CHUNKS,)),
        ],
        compiler_params=pltpu.CompilerParams(
            collective_id=0, has_side_effects=True, vmem_limit_bytes=58 * 1024 * 1024),
        name="pair",
    )(*operands)


def solution(mesh):
    axes = tuple(mesh.axis_names)
    placed = (P(axes, None), P(), P(), P(), P())
    return jax.shard_map(
        functools.partial(on_device, axes),
        mesh=mesh,
        in_specs=placed,
        out_specs=P(axes, None),
        check_vma=False,
    )
```

```python
import functools

import jax
import jax.numpy as jnp
from jax import lax
from jax.experimental import pallas as pl
from jax.experimental.pallas import tpu as pltpu
from jax.sharding import PartitionSpec as P

F32 = jnp.float32
BF16 = jnp.bfloat16
LANES = 128
CHUNKS = 16
EARLY = 4
SIDE = 2
STEP = 4
LEAD = 16
NEAR = 10
SLICES = 8
MESH = pl.DeviceIdType.MESH


def lanes_of(c, width=LANES):
    return pl.ds(pl.multiple_of(c * width, width), width)


def row_scale(total, channels):
    mean = jnp.sum(total, axis=-1, keepdims=True) * (1.0 / channels)
    return jnp.broadcast_to(lax.rsqrt(mean + 1e-06), total.shape)


def square_sums(read, rows, blocks):
    def add(c, total):
        v = read(c).astype(F32)
        return total + v * v

    return lax.fori_loop(0, blocks, add, jnp.zeros((rows, LANES), F32))


def stream(z_ref, taps, first, rows):
    total = taps[0] * z_ref[8 + first : 8 + first + rows]
    for i in range(1, len(taps)):
        total = total + taps[i] * z_ref[8 + first - i : 8 + first - i + rows]
    return total


def feat_rows(feat_ref, o, gain, cs):
    streams, feat = feat_ref.shape[1:3]
    return [[feat_ref[0, j, i, o : o + 1, cs] * gain for i in range(feat)] for j in range(streams)]


def pieces(rows, most=48):
    return [(first, min(most, rows - first)) for first in range(0, rows, most)]


def short_block(c, read, rows, gain_ref, feat_ref, taps_ref, z_ref, w_ref, s_ref, h_ref, start, hs):
    cs = lanes_of(c)
    gain = gain_ref[0, 0:1, cs]
    taps = feat_rows(feat_ref, 0, gain, cs)
    short = [taps_ref[i, 0:1, cs] for i in range(taps_ref.shape[0])]
    z_ref[8 : 8 + rows] = read(c).astype(F32) * s_ref[:rows]
    for first, count in pieces(rows):
        u1 = stream(z_ref, taps[1], first, count)
        u2 = stream(z_ref, taps[2], first, count)
        w_ref[8 + first : 8 + first + count] = (u1 * u2).astype(BF16).astype(F32)
    for first, count in pieces(rows):
        f = stream(w_ref, short, first, count)
        u0 = stream(z_ref, taps[0], first, count)
        h_ref[start + first : start + first + count, hs] = u0 * f
    h = (h_ref[start : start + rows, hs] + read(c).astype(F32)).astype(BF16).astype(F32)
    h_ref[start : start + rows, hs] = h
    return h


def same_place(rows):
    return (lax.broadcasted_iota(jnp.int32, (rows, LANES), 0)
            == lax.broadcasted_iota(jnp.int32, (rows, LANES), 1))


def pack_rows(values_ref, start, rows, pack_ref):
    for r, (first, count) in enumerate(pieces(rows, LANES)):
        values = values_ref[start + first : start + first + count]
        pack_ref[r : r + 1] = jnp.sum(jnp.where(same_place(count), values, 0.0), axis=0, keepdims=True)


def unpack_rows(pack_ref, rows, values_ref):
    for r, (first, count) in enumerate(pieces(rows, LANES)):
        values = jnp.broadcast_to(pack_ref[r : r + 1], (count, LANES))
        column = jnp.sum(jnp.where(same_place(count), values, 0.0), axis=1, keepdims=True)
        values_ref[first : first + count] = jnp.broadcast_to(column, (count, LANES))


def kernel(axes, x_hbm, gain_hbm, feat_hbm, taps_hbm, mr_hbm, out_ref,
           x_ref, gain_ref, feat_ref, taps_ref, mr_ref,
           lead_ref, win_ref, h_ref, u_ref, table_ref, base_ref, rhs_ref, scale_ref, z_ref, w_ref,
           s_ref, sum_ref, halo_ref, told_ref, before_ref, give_ref, got_ref, near_ref, near_give_ref, near_got_ref, relay_ref,
           local_sems, lead_sems, send_sems, recv_sems, relay_send_sems, relay_recv_sems,
           side_ref, side_send_sems, side_recv_sems):
    rows, channels = x_ref.shape
    tap_count, group_count = mr_ref.shape[1:]
    per_group = channels // group_count
    groups = LANES // per_group
    half = rows // 2
    blocks = channels // LANES
    part = channels // CHUNKS
    here = blocks // CHUNKS
    tail = tap_count + LEAD
    first_tail = rows - tail
    first_sent = rows - tap_count
    early_width = EARLY * part
    near_width = (channels - early_width) // SLICES
    outer, inner = axes
    inner_size = lax.axis_size(inner)
    count = lax.axis_size(outer) * inner_size
    me = lax.axis_index(outer) * inner_size + lax.axis_index(inner)
    behind, ahead = me - 1, me + 1
    has_behind, has_ahead = me > 0, me < count - 1
    sections, section = lax.axis_size(outer), lax.axis_index(outer)
    start_of, end_of = lax.axis_index(inner) == 0, lax.axis_index(inner) == inner_size - 1
    odd, even = section % 2 == 1, section % 2 == 0
    via_relay = end_of & odd & (section + 2 < sections)
    is_relay = end_of & odd & (section >= 3)
    is_side = start_of & even & (section + 3 < sections)
    past_relay = start_of & even & (section >= 2) & (section + 1 < sections)

    def place(index):
        return (index // inner_size, index % inner_size)

    barrier = pltpu.get_barrier_semaphore()

    @pl.when(has_behind)
    def _():
        pl.semaphore_signal(barrier, inc=1, device_id=place(behind), device_id_type=MESH)

    @pl.when(is_relay)
    def _():
        pl.semaphore_signal(barrier, inc=1, device_id=place(me - 2 * inner_size), device_id_type=MESH)

    @pl.when(is_side)
    def _():
        pl.semaphore_signal(barrier, inc=1, device_id=place(behind + 2 * inner_size), device_id_type=MESH)

    @pl.when(past_relay)
    def _():
        pl.semaphore_signal(barrier, inc=1, device_id=place(me - 2 * inner_size), device_id_type=MESH)
        pl.semaphore_signal(barrier, inc=1, device_id=place(behind + 2 * inner_size), device_id_type=MESH)

    loads = [pltpu.make_async_copy(src, dst, local_sems.at[i]) for i, (src, dst) in enumerate(
        [(x_hbm, x_ref), (gain_hbm, gain_ref), (feat_hbm, feat_ref), (taps_hbm, taps_ref), (mr_hbm, mr_ref)])]
    for load in loads:
        load.start()

    def to_device(index, src, dst, send_sem, recv_sem):
        return pltpu.make_async_remote_copy(
            src_ref=src, dst_ref=dst, send_sem=send_sem, recv_sem=recv_sem,
            device_id=place(index), device_id_type=MESH)

    to_ahead = functools.partial(to_device, ahead)

    def lead_copy():
        cs = slice(0, early_width)
        return to_ahead(x_hbm.at[pl.ds(rows - LEAD, LEAD), cs], lead_ref, lead_sems.at[0], lead_sems.at[1])

    def near_copy():
        return to_ahead(near_give_ref, near_got_ref, lead_sems.at[6], lead_sems.at[7])

    def tell_copy(o):
        return to_ahead(give_ref.at[o], got_ref.at[o], lead_sems.at[2 + 2 * o], lead_sems.at[3 + 2 * o])

    def early_copy(k):
        cs = lanes_of(k, part)
        return to_ahead(x_hbm.at[pl.ds(first_tail, tap_count), cs], win_ref.at[pl.ds(0, tap_count), cs],
                        send_sems.at[k], recv_sems.at[k])

    def part_copy(k):
        cs = lanes_of(k, part)
        return to_ahead(win_ref.at[pl.ds(rows, tap_count), cs], win_ref.at[pl.ds(0, tap_count), cs],
                        send_sems.at[k], recv_sems.at[k])

    def to_relay_copy(k):
        cs = lanes_of(k, part)
        return to_device(me + 2 * inner_size, x_hbm.at[pl.ds(first_tail, tap_count), cs], relay_ref.at[:, cs],
                         send_sems.at[k], relay_recv_sems.at[k])

    def from_relay_copy(k):
        cs = lanes_of(k, part)
        return to_device(me - 2 * inner_size + 1, relay_ref.at[:, cs], win_ref.at[pl.ds(0, tap_count), cs],
                         relay_send_sems.at[k], recv_sems.at[k])

    def side_columns(k):
        return lanes_of(k - EARLY, part)

    def to_side_copy(k):
        return to_device(ahead - 2 * inner_size, win_ref.at[pl.ds(rows, tap_count), lanes_of(k, part)],
                         side_ref.at[:, side_columns(k)], send_sems.at[k], side_recv_sems.at[k - EARLY])

    def from_side_copy(k):
        return to_device(me + 2 * inner_size, side_ref.at[:, side_columns(k)],
                         win_ref.at[pl.ds(0, tap_count), lanes_of(k, part)],
                         side_send_sems.at[k - EARLY], recv_sems.at[k])

    greeted = [has_ahead, via_relay, via_relay, is_relay, is_side]
    pl.semaphore_wait(barrier, sum(g.astype(jnp.int32) for g in greeted))

    @pl.when(has_ahead)
    def _():
        lead_copy().start()

    @pl.when(has_ahead & jnp.logical_not(via_relay))
    def _():
        @pl.loop(0, EARLY)
        def _(k):
            early_copy(k).start()

    @pl.when(via_relay)
    def _():
        @pl.loop(0, EARLY)
        def _(k):
            to_relay_copy(k).start()

    z_ref[...] = jnp.zeros_like(z_ref)
    w_ref[...] = jnp.zeros_like(w_ref)
    give_ref[...] = jnp.zeros_like(give_ref)
    share = (gain_ref, feat_ref, taps_ref, z_ref, w_ref, s_ref)
    early_blocks = EARLY * here

    def mr_product(taps, first, size):
        return (stream(z_ref, taps[1], first, size) * stream(z_ref, taps[2], first, size)).astype(BF16)

    def mr_taps_of(cs):
        return feat_rows(feat_ref, 1, gain_ref[0, 1:2, cs], cs)

    loads[0].wait()
    for i in range(SLICES):
        cs = slice(early_width + i * near_width, early_width + (i + 1) * near_width)
        near_ref[i * NEAR : (i + 1) * NEAR] = x_ref[rows - LEAD :, cs].astype(F32)[LEAD - NEAR :]
    near_give_ref[...] = near_ref[...].astype(BF16)

    @pl.when(has_ahead)
    def _():
        near_copy().start()

    read_tail = lambda c: x_ref[first_tail:, lanes_of(c)]
    s_ref[:tail] = row_scale(square_sums(read_tail, tail, blocks), channels)
    pack_rows(s_ref, 0, tail, give_ref.at[0])

    @pl.when(has_ahead)
    def _():
        tell_copy(0).start()

    for load in loads[1:]:
        load.wait()
    sum_ref[:tail] = jnp.zeros((tail, LANES), F32)
    start_tail = LEAD + first_tail

    @pl.loop(0, blocks)
    def _(c):
        h = short_block(c, read_tail, tail, *share, h_ref, start_tail, lanes_of(c))
        sum_ref[:tail] += h * h

    scale_ref[start_tail : start_tail + tail] = row_scale(sum_ref[:tail], channels)
    pack_rows(scale_ref, start_tail, tail, give_ref.at[1])

    @pl.when(has_ahead)
    def _():
        tell_copy(1).start()

    @pl.loop(EARLY, CHUNKS)
    def _(k):
        @pl.loop(0, here)
        def _(b):
            cs = lanes_of(k * here + b)
            taps = mr_taps_of(cs)
            n = tap_count + 8
            top = LEAD + first_sent - 8
            z_ref[0:n] = h_ref[top : top + n, cs] * scale_ref[top : top + n]
            for first, size in pieces(tap_count):
                win_ref[rows + first : rows + first + size, cs] = mr_product(taps, first, size)

        beside = via_relay & (k < EARLY + SIDE)

        @pl.when(has_ahead & jnp.logical_not(beside))
        def _():
            part_copy(k).start()

        @pl.when(beside)
        def _():
            to_side_copy(k).start()

    @pl.when(is_relay)
    def _():
        @pl.loop(0, EARLY)
        def _(k):
            to_relay_copy(k).wait_recv()
            from_relay_copy(k).start()

    at_tap = lax.broadcasted_iota(jnp.int32, (tap_count, tap_count), 0)
    at_lag = lax.broadcasted_iota(jnp.int32, (tap_count, tap_count), 1)
    flip = jnp.where((at_tap + at_lag == tap_count) | (at_tap + at_lag == 0), 1.0, 0.0).astype(BF16)
    past = (lax.broadcasted_iota(jnp.int32, (half, tap_count), 1)
            > lax.broadcasted_iota(jnp.int32, (half, tap_count), 0))
    base_ref[...] = lax.dot_general(mr_ref[0], flip, (((0,), (0,)), ((), ())),
                                    preferred_element_type=F32)
    rhs_ref[...] = jnp.zeros_like(rhs_ref)

    @pl.when(has_behind)
    def _():
        lead_copy().wait_recv()
        near_copy().wait_recv()

    @pl.when(jnp.logical_not(has_behind))
    def _():
        lead_ref[...] = jnp.zeros_like(lead_ref)
        near_got_ref[...] = jnp.zeros_like(near_got_ref)
        win_ref[:tap_count] = jnp.zeros((tap_count, channels), BF16)

    before_ref[:, :early_width] = lead_ref[...].astype(F32)
    near_ref[...] = near_got_ref[...].astype(F32)
    for i in range(SLICES):
        cs = slice(early_width + i * near_width, early_width + (i + 1) * near_width)
        before_ref[: LEAD - NEAR, cs] = jnp.zeros((LEAD - NEAR, near_width), F32)
        before_ref[LEAD - NEAR :, cs] = near_ref[i * NEAR : (i + 1) * NEAR]

    head = LEAD + first_sent
    z_ref[0:8] = jnp.zeros((8, LANES), F32)
    read_head = lambda c: jnp.concatenate(
        [before_ref[:, lanes_of(c)], x_ref[:first_sent, lanes_of(c)].astype(F32)], axis=0)
    s_ref[:head] = row_scale(square_sums(read_head, head, blocks), channels)
    sum_ref[:head] = jnp.zeros((head, LANES), F32)

    @pl.loop(0, blocks)
    def _(c):
        h = short_block(c, read_head, head, *share, h_ref, 0, lanes_of(c))
        sum_ref[:head] += h * h

    scale_ref[:head] = row_scale(sum_ref[:head], channels)

    @pl.loop(0, blocks)
    def _(c):
        cs = lanes_of(c)
        taps = mr_taps_of(cs)
        z_ref[0 : rows + 8] = h_ref[LEAD - 8 :, cs] * scale_ref[LEAD - 8 :]

        def put(low, high):
            for first, size in pieces(high - low):
                first += low
                win_ref[tap_count + first : tap_count + first + size, cs] = mr_product(taps, first, size)

        put(0, first_sent)

        @pl.when(c < early_blocks)
        def _():
            put(first_sent, rows)

        for first, size in pieces(rows):
            u_ref[first : first + size, cs] = stream(z_ref, taps[0], first, size)

    @pl.when(is_side)
    def _():
        @pl.loop(EARLY, EARLY + SIDE)
        def _(k):
            to_side_copy(k).wait_recv()
            from_side_copy(k).start()

    @pl.loop(0, blocks)
    def _(c):
        lags = base_ref[pl.ds(pl.multiple_of(c * groups, groups), groups), :]
        for g in range(groups):
            row = jnp.broadcast_to(lags[g : g + 1], (half, tap_count))
            turned = pltpu.roll(row, 0, 1, stride=1, stride_axis=0)
            gs = slice(g * half, (g + 1) * half)
            table_ref[c, gs, :tap_count] = jnp.where(past, turned, 0.0).astype(BF16)
            table_ref[c, gs, tap_count:] = jnp.where(past, 0.0, turned).astype(BF16)

    lane_group = lax.broadcasted_iota(jnp.int32, (half, LANES), 1) // per_group
    reach = half + tap_count

    @pl.when(has_behind)
    def _():
        tell_copy(0).wait_recv()
        unpack_rows(got_ref.at[0], tail, s_ref)
        tell_copy(1).wait_recv()
        unpack_rows(got_ref.at[1], tail, told_ref)

    @pl.loop(0, CHUNKS)
    def _(k):
        @pl.when(has_behind)
        def _():
            part_copy(k).wait_recv()

        @pl.when(has_behind & (k < EARLY))
        def _():
            @pl.loop(0, here)
            def _(b):
                c = k * here + b
                cs = lanes_of(c)
                read_halo = lambda _: jnp.concatenate([win_ref[:tap_count, cs].astype(F32), before_ref[:, cs]], axis=0)
                short_block(c, read_halo, tail, *share, halo_ref, 0, slice(None))
                taps = mr_taps_of(cs)
                z_ref[0:tail] = halo_ref[...] * told_ref[...]
                for first, size in pieces(tap_count):
                    win_ref[first : first + size, cs] = mr_product(taps, tail - tap_count - 8 + first, size)

        @pl.loop(0, here, step=STEP)
        def _(b):
          for slot in range(STEP):
            c = k * here + b + slot
            cs = lanes_of(c)
            rhs_ref[slot, :reach, :LANES] = win_ref[:reach, cs]
            rhs_ref[slot, :reach, LANES:] = win_ref[half : half + reach, cs]
            product = jnp.dot(table_ref[c], rhs_ref[slot], preferred_element_type=F32)
            for side in range(2):
                ls = slice(side * LANES, (side + 1) * LANES)
                f = product[0:half, ls]
                for g in range(1, groups):
                    f = jnp.where(lane_group == g, product[g * half : (g + 1) * half, ls], f)
                rs = slice(side * half, (side + 1) * half)
                hs = slice(LEAD + side * half, LEAD + (side + 1) * half)
                out_ref[rs, cs] = (h_ref[hs, cs] + u_ref[rs, cs] * f).astype(BF16)

    @pl.when(has_ahead)
    def _():
        lead_copy().wait_send()
        near_copy().wait_send()
        tell_copy(0).wait_send()
        tell_copy(1).wait_send()

        @pl.loop(0, CHUNKS)
        def _(k):
            part_copy(k).wait_send()

    @pl.when(is_relay)
    def _():
        @pl.loop(0, EARLY)
        def _(k):
            from_relay_copy(k).wait_send()

    @pl.when(is_side)
    def _():
        @pl.loop(EARLY, EARLY + SIDE)
        def _(k):
            from_side_copy(k).wait_send()


def on_device(axes, tokens, norm_gain, feat_taps, se_taps, mr_taps):
    rows, channels = tokens.shape
    tap_count, group_count = mr_taps.shape[1:]
    groups = LANES * group_count // channels
    blocks = channels // LANES
    spread = 2 * tap_count
    early_width = EARLY * channels // CHUNKS
    near_width = (channels - early_width) // SLICES
    operands = (tokens, norm_gain, feat_taps.transpose(0, 2, 3, 1, 4), se_taps.transpose(1, 0, 2), mr_taps)
    return pl.pallas_call(
        functools.partial(kernel, axes),
        out_shape=pltpu.VMEM((rows, channels), BF16),
        in_specs=[pl.BlockSpec(memory_space=pltpu.HBM)] * 5,
        out_specs=pl.BlockSpec(memory_space=pltpu.VMEM),
        scratch_shapes=[pltpu.VMEM(a.shape, a.dtype) for a in operands] + [
            pltpu.VMEM((LEAD, early_width), BF16),
            pltpu.VMEM((tap_count + rows, channels), BF16),
            pltpu.VMEM((LEAD + rows, channels), F32),
            pltpu.VMEM((rows, channels), F32),
            pltpu.VMEM((blocks, groups * rows // 2, spread), BF16),
            pltpu.VMEM((group_count, tap_count), F32),
            pltpu.VMEM((STEP, spread, 2 * LANES), BF16),
            pltpu.VMEM((LEAD + rows, LANES), F32),
            pltpu.VMEM((LEAD + rows, LANES), F32),
            pltpu.VMEM((LEAD + rows, LANES), F32),
            pltpu.VMEM((LEAD + rows, LANES), F32),
            pltpu.VMEM((LEAD + rows, LANES), F32),
            pltpu.VMEM((tap_count + LEAD, LANES), F32),
            pltpu.VMEM((tap_count + LEAD, LANES), F32),
            pltpu.VMEM((LEAD, channels), F32),
            pltpu.VMEM((2, 8, LANES), F32),
            pltpu.VMEM((2, 8, LANES), F32),
            pltpu.VMEM((SLICES * NEAR, near_width), F32),
            pltpu.VMEM((SLICES * NEAR, near_width), BF16),
            pltpu.VMEM((SLICES * NEAR, near_width), BF16),
            pltpu.VMEM((tap_count, early_width), BF16),
            pltpu.SemaphoreType.DMA((5,)),
            pltpu.SemaphoreType.DMA((8,)),
            pltpu.SemaphoreType.DMA((CHUNKS,)),
            pltpu.SemaphoreType.DMA((CHUNKS,)),
            pltpu.SemaphoreType.DMA((EARLY,)),
            pltpu.SemaphoreType.DMA((EARLY,)),
            pltpu.VMEM((tap_count, SIDE * channels // CHUNKS), BF16),
            pltpu.SemaphoreType.DMA((SIDE,)),
            pltpu.SemaphoreType.DMA((SIDE,)),
        ],
        compiler_params=pltpu.CompilerParams(
            collective_id=0, has_side_effects=True, vmem_limit_bytes=58 * 1024 * 1024),
        name="pair",
    )(*operands)


def solution(mesh):
    axes = tuple(mesh.axis_names)
    placed = (P(axes, None), P(), P(), P(), P())
    return jax.shard_map(
        functools.partial(on_device, axes),
        mesh=mesh,
        in_specs=placed,
        out_specs=P(axes, None),
        check_vma=False,
    )
```

```python
import functools

import jax
import jax.numpy as jnp
from jax import lax
from jax.experimental import pallas as pl
from jax.experimental.pallas import tpu as pltpu
from jax.sharding import PartitionSpec as P

F32 = jnp.float32
BF16 = jnp.bfloat16
LANES = 128
CHUNKS = 16
EARLY = 4
SIDE = 4
STEP = 4
LEAD = 16
NEAR = 10
SLICES = 8
MESH = pl.DeviceIdType.MESH


def lanes_of(c, width=LANES):
    return pl.ds(pl.multiple_of(c * width, width), width)


def row_scale(total, channels):
    mean = jnp.sum(total, axis=-1, keepdims=True) * (1.0 / channels)
    return jnp.broadcast_to(lax.rsqrt(mean + 1e-06), total.shape)


def square_sums(read, rows, blocks):
    def add(c, total):
        v = read(c).astype(F32)
        return total + v * v

    return lax.fori_loop(0, blocks, add, jnp.zeros((rows, LANES), F32))


def stream(z_ref, taps, first, rows):
    total = taps[0] * z_ref[8 + first : 8 + first + rows]
    for i in range(1, len(taps)):
        total = total + taps[i] * z_ref[8 + first - i : 8 + first - i + rows]
    return total


def feat_rows(feat_ref, o, gain, cs):
    streams, feat = feat_ref.shape[1:3]
    return [[feat_ref[0, j, i, o : o + 1, cs] * gain for i in range(feat)] for j in range(streams)]


def pieces(rows, most=48):
    return [(first, min(most, rows - first)) for first in range(0, rows, most)]


def short_block(c, read, rows, gain_ref, feat_ref, taps_ref, z_ref, w_ref, s_ref, h_ref, start, hs):
    cs = lanes_of(c)
    gain = gain_ref[0, 0:1, cs]
    taps = feat_rows(feat_ref, 0, gain, cs)
    short = [taps_ref[i, 0:1, cs] for i in range(taps_ref.shape[0])]
    z_ref[8 : 8 + rows] = read(c).astype(F32) * s_ref[:rows]
    for first, count in pieces(rows):
        u1 = stream(z_ref, taps[1], first, count)
        u2 = stream(z_ref, taps[2], first, count)
        w_ref[8 + first : 8 + first + count] = (u1 * u2).astype(BF16).astype(F32)
    for first, count in pieces(rows):
        f = stream(w_ref, short, first, count)
        u0 = stream(z_ref, taps[0], first, count)
        h_ref[start + first : start + first + count, hs] = u0 * f
    h = (h_ref[start : start + rows, hs] + read(c).astype(F32)).astype(BF16).astype(F32)
    h_ref[start : start + rows, hs] = h
    return h


def same_place(rows):
    return (lax.broadcasted_iota(jnp.int32, (rows, LANES), 0)
            == lax.broadcasted_iota(jnp.int32, (rows, LANES), 1))


def pack_rows(values_ref, start, rows, pack_ref):
    for r, (first, count) in enumerate(pieces(rows, LANES)):
        values = values_ref[start + first : start + first + count]
        pack_ref[r : r + 1] = jnp.sum(jnp.where(same_place(count), values, 0.0), axis=0, keepdims=True)


def unpack_rows(pack_ref, rows, values_ref):
    for r, (first, count) in enumerate(pieces(rows, LANES)):
        values = jnp.broadcast_to(pack_ref[r : r + 1], (count, LANES))
        column = jnp.sum(jnp.where(same_place(count), values, 0.0), axis=1, keepdims=True)
        values_ref[first : first + count] = jnp.broadcast_to(column, (count, LANES))


def kernel(axes, x_hbm, gain_hbm, feat_hbm, taps_hbm, mr_hbm, out_ref,
           x_ref, gain_ref, feat_ref, taps_ref, mr_ref,
           stage_ref, win_ref, h_ref, u_ref, table_ref, base_ref, rhs_ref, scale_ref, z_ref, w_ref,
           s_ref, sum_ref, halo_ref, behind_ref, told_ref, before_ref, give_ref, got_ref, near_ref, near_give_ref, near_got_ref, relay_ref,
           local_sems, lead_sems, send_sems, recv_sems, relay_send_sems, relay_recv_sems,
           side_ref, side_send_sems, side_recv_sems, last_send_sems, last_recv_sems):
    rows, channels = x_ref.shape
    tap_count, group_count = mr_ref.shape[1:]
    per_group = channels // group_count
    groups = LANES // per_group
    half = rows // 2
    blocks = channels // LANES
    part = channels // CHUNKS
    here = blocks // CHUNKS
    tail = tap_count + LEAD
    first_tail = rows - tail
    first_sent = rows - tap_count
    early_width = EARLY * part
    near_width = channels // SLICES
    far = LEAD - NEAR
    last_chunk = CHUNKS - 1
    outer, inner = axes
    inner_size = lax.axis_size(inner)
    count = lax.axis_size(outer) * inner_size
    me = lax.axis_index(outer) * inner_size + lax.axis_index(inner)
    behind, ahead = me - 1, me + 1
    has_behind, has_ahead = me > 0, me < count - 1
    sections, section = lax.axis_size(outer), lax.axis_index(outer)
    start_of, end_of = lax.axis_index(inner) == 0, lax.axis_index(inner) == inner_size - 1
    odd, even = section % 2 == 1, section % 2 == 0
    via_relay = end_of & odd & (section + 2 < sections)
    is_relay = end_of & odd & (section >= 3)
    is_side = start_of & even & (section + 3 < sections)
    past_relay = start_of & even & (section >= 2) & (section + 1 < sections)

    def place(index):
        return (index // inner_size, index % inner_size)

    barrier = pltpu.get_barrier_semaphore()

    @pl.when(has_behind)
    def _():
        pl.semaphore_signal(barrier, inc=1, device_id=place(behind), device_id_type=MESH)

    @pl.when(is_relay)
    def _():
        pl.semaphore_signal(barrier, inc=1, device_id=place(me - 2 * inner_size), device_id_type=MESH)

    @pl.when(is_side)
    def _():
        pl.semaphore_signal(barrier, inc=1, device_id=place(behind + 2 * inner_size), device_id_type=MESH)

    @pl.when(past_relay)
    def _():
        pl.semaphore_signal(barrier, inc=1, device_id=place(me - 2 * inner_size), device_id_type=MESH)
        pl.semaphore_signal(barrier, inc=1, device_id=place(behind + 2 * inner_size), device_id_type=MESH)

    loads = [pltpu.make_async_copy(src, dst, local_sems.at[i]) for i, (src, dst) in enumerate(
        [(x_hbm.at[pl.ds(rows - LEAD, LEAD)], x_ref.at[pl.ds(rows - LEAD, LEAD)]),
         (x_hbm.at[pl.ds(0, rows - LEAD)], x_ref.at[pl.ds(0, rows - LEAD)]), (gain_hbm, gain_ref), (feat_hbm, feat_ref), (taps_hbm, taps_ref), (mr_hbm, mr_ref)])]
    for load in loads:
        load.start()

    def to_device(index, src, dst, send_sem, recv_sem):
        return pltpu.make_async_remote_copy(
            src_ref=src, dst_ref=dst, send_sem=send_sem, recv_sem=recv_sem,
            device_id=place(index), device_id_type=MESH)

    to_ahead = functools.partial(to_device, ahead)

    def near_copy():
        return to_ahead(near_give_ref, near_got_ref, lead_sems.at[0], lead_sems.at[1])

    def tell_copy(o):
        return to_ahead(give_ref.at[o], got_ref.at[o], lead_sems.at[2 + 2 * o], lead_sems.at[3 + 2 * o])

    def early_copy(k):
        cs = lanes_of(k, part)
        return to_ahead(stage_ref.at[:, cs], win_ref.at[pl.ds(0, tap_count), cs],
                        send_sems.at[k], recv_sems.at[k])

    def part_copy(k):
        cs = lanes_of(k, part)
        return to_ahead(win_ref.at[pl.ds(rows, tap_count), cs], win_ref.at[pl.ds(0, tap_count), cs],
                        send_sems.at[k], recv_sems.at[k])

    def to_relay_copy(k):
        cs = lanes_of(k, part)
        return to_device(me + 2 * inner_size, stage_ref.at[:, cs], relay_ref.at[:, cs],
                         send_sems.at[k], relay_recv_sems.at[k])

    def from_relay_copy(k):
        cs = lanes_of(k, part)
        return to_device(me - 2 * inner_size + 1, relay_ref.at[:, cs], win_ref.at[pl.ds(0, tap_count), cs],
                         relay_send_sems.at[k], recv_sems.at[k])

    def side_columns(k):
        return lanes_of(k - EARLY, part)

    def to_side_copy(k):
        return to_device(ahead - 2 * inner_size, win_ref.at[pl.ds(rows, tap_count), lanes_of(k, part)],
                         side_ref.at[:, side_columns(k)], send_sems.at[k], side_recv_sems.at[k - EARLY])

    def from_side_copy(k):
        return to_device(me + 2 * inner_size, side_ref.at[:, side_columns(k)],
                         win_ref.at[pl.ds(0, tap_count), lanes_of(k, part)],
                         side_send_sems.at[k - EARLY], recv_sems.at[k])


    def last_copy(b):
        cs = lanes_of(last_chunk * here + b)
        return to_ahead(win_ref.at[pl.ds(rows, tap_count), cs], win_ref.at[pl.ds(0, tap_count), cs],
                        last_send_sems.at[b], last_recv_sems.at[b])

    loads[0].wait()
    for i in range(SLICES):
        cs = slice(i * near_width, (i + 1) * near_width)
        near_ref[i * NEAR : (i + 1) * NEAR] = x_ref[rows - LEAD :, cs].astype(F32)[far:]
    near_give_ref[...] = near_ref[...].astype(BF16)
    greeted = [has_ahead, via_relay, via_relay, is_relay, is_side]
    pl.semaphore_wait(barrier, sum(g.astype(jnp.int32) for g in greeted))

    @pl.when(has_ahead)
    def _():
        near_copy().start()

    loads[1].wait()

    @pl.loop(0, EARLY)
    def _(k):
        @pl.loop(0, here)
        def _(b):
            cs = lanes_of(k * here + b)
            stage_ref[:, cs] = x_ref[first_tail:, cs].astype(F32)[far : far + tap_count].astype(BF16)

        @pl.when(has_ahead & jnp.logical_not(via_relay))
        def _():
            early_copy(k).start()

        @pl.when(via_relay)
        def _():
            to_relay_copy(k).start()

    z_ref[...] = jnp.zeros_like(z_ref)
    w_ref[...] = jnp.zeros_like(w_ref)
    give_ref[...] = jnp.zeros_like(give_ref)
    share = (gain_ref, feat_ref, taps_ref, z_ref, w_ref, s_ref)
    early_blocks = EARLY * here

    def mr_product(taps, first, size):
        return (stream(z_ref, taps[1], first, size) * stream(z_ref, taps[2], first, size)).astype(BF16)

    def mr_taps_of(cs):
        return feat_rows(feat_ref, 1, gain_ref[0, 1:2, cs], cs)

    read_tail = lambda c: x_ref[first_tail:, lanes_of(c)]
    s_ref[:tail] = row_scale(square_sums(read_tail, tail, blocks), channels)
    pack_rows(s_ref, 0, tail, give_ref.at[0])

    @pl.when(has_ahead)
    def _():
        tell_copy(0).start()

    for load in loads[2:]:
        load.wait()
    sum_ref[:tail] = jnp.zeros((tail, LANES), F32)
    start_tail = LEAD + first_tail

    @pl.loop(0, blocks)
    def _(c):
        h = short_block(c, read_tail, tail, *share, h_ref, start_tail, lanes_of(c))
        sum_ref[:tail] += h * h

    scale_ref[start_tail : start_tail + tail] = row_scale(sum_ref[:tail], channels)
    pack_rows(scale_ref, start_tail, tail, give_ref.at[1])

    @pl.when(has_ahead)
    def _():
        tell_copy(1).start()

    def product_to_send(c):
        cs = lanes_of(c)
        taps = mr_taps_of(cs)
        n = tap_count + 8
        top = LEAD + first_sent - 8
        z_ref[0:n] = h_ref[top : top + n, cs] * scale_ref[top : top + n]
        for first, size in pieces(tap_count):
            win_ref[rows + first : rows + first + size, cs] = mr_product(taps, first, size)

    @pl.loop(EARLY, last_chunk)
    def _(k):
        @pl.loop(0, here)
        def _(b):
            product_to_send(k * here + b)

        beside = via_relay & (k < EARLY + SIDE)

        @pl.when(has_ahead & jnp.logical_not(beside))
        def _():
            part_copy(k).start()

        @pl.when(beside)
        def _():
            to_side_copy(k).start()

    @pl.loop(0, here)
    def _(b):
        product_to_send(last_chunk * here + b)

        @pl.when(has_ahead)
        def _():
            last_copy(b).start()

    @pl.when(is_relay)
    def _():
        @pl.loop(0, EARLY)
        def _(k):
            to_relay_copy(k).wait_recv()
            from_relay_copy(k).start()

    at_tap = lax.broadcasted_iota(jnp.int32, (tap_count, tap_count), 0)
    at_lag = lax.broadcasted_iota(jnp.int32, (tap_count, tap_count), 1)
    flip = jnp.where((at_tap + at_lag == tap_count) | (at_tap + at_lag == 0), 1.0, 0.0).astype(BF16)
    past = (lax.broadcasted_iota(jnp.int32, (half, tap_count), 1)
            > lax.broadcasted_iota(jnp.int32, (half, tap_count), 0))
    base_ref[...] = lax.dot_general(mr_ref[0], flip, (((0,), (0,)), ((), ())),
                                    preferred_element_type=F32)
    rhs_ref[...] = jnp.zeros_like(rhs_ref)

    @pl.when(has_behind)
    def _():
        near_copy().wait_recv()

    @pl.when(jnp.logical_not(has_behind))
    def _():
        near_got_ref[...] = jnp.zeros_like(near_got_ref)
        win_ref[:tap_count] = jnp.zeros((tap_count, channels), BF16)

    near_ref[...] = near_got_ref[...].astype(F32)
    for i in range(SLICES):
        cs = slice(i * near_width, (i + 1) * near_width)
        before_ref[:far, cs] = jnp.zeros((far, near_width), F32)
        before_ref[far:, cs] = near_ref[i * NEAR : (i + 1) * NEAR]

    head = LEAD + first_sent
    z_ref[0:8] = jnp.zeros((8, LANES), F32)
    read_head = lambda c: jnp.concatenate(
        [before_ref[:, lanes_of(c)], x_ref[:first_sent, lanes_of(c)].astype(F32)], axis=0)
    s_ref[:head] = row_scale(square_sums(read_head, head, blocks), channels)
    sum_ref[:head] = jnp.zeros((head, LANES), F32)

    @pl.loop(0, blocks)
    def _(c):
        h = short_block(c, read_head, head, *share, h_ref, 0, lanes_of(c))
        sum_ref[:head] += h * h

    scale_ref[:head] = row_scale(sum_ref[:head], channels)

    @pl.loop(0, blocks)
    def _(c):
        cs = lanes_of(c)
        taps = mr_taps_of(cs)
        z_ref[0 : rows + 8] = h_ref[LEAD - 8 :, cs] * scale_ref[LEAD - 8 :]

        def put(low, high):
            for first, size in pieces(high - low):
                first += low
                win_ref[tap_count + first : tap_count + first + size, cs] = mr_product(taps, first, size)

        put(0, first_sent)

        @pl.when(c < early_blocks)
        def _():
            put(first_sent, rows)

        for first, size in pieces(rows):
            u_ref[first : first + size, cs] = stream(z_ref, taps[0], first, size)

    @pl.when(is_side)
    def _():
        @pl.loop(EARLY, EARLY + SIDE)
        def _(k):
            to_side_copy(k).wait_recv()
            from_side_copy(k).start()

    @pl.loop(0, blocks)
    def _(c):
        lags = base_ref[pl.ds(pl.multiple_of(c * groups, groups), groups), :]
        for g in range(groups):
            row = jnp.broadcast_to(lags[g : g + 1], (half, tap_count))
            turned = pltpu.roll(row, 0, 1, stride=1, stride_axis=0)
            gs = slice(g * half, (g + 1) * half)
            table_ref[c, gs, :tap_count] = jnp.where(past, turned, 0.0).astype(BF16)
            table_ref[c, gs, tap_count:] = jnp.where(past, 0.0, turned).astype(BF16)

    lane_group = lax.broadcasted_iota(jnp.int32, (half, LANES), 1) // per_group
    reach = half + tap_count

    @pl.when(has_behind)
    def _():
        tell_copy(0).wait_recv()
        unpack_rows(got_ref.at[0], tail, s_ref)
        tell_copy(1).wait_recv()
        unpack_rows(got_ref.at[1], tail, told_ref)

    behind_ref[:far] = jnp.zeros((far, LANES), F32)

    def finish(c, slot):
        cs = lanes_of(c)
        rhs_ref[slot, :reach, :LANES] = win_ref[:reach, cs]
        rhs_ref[slot, :reach, LANES:] = win_ref[half : half + reach, cs]
        product = jnp.dot(table_ref[c], rhs_ref[slot], preferred_element_type=F32)
        for side in range(2):
            ls = slice(side * LANES, (side + 1) * LANES)
            f = product[0:half, ls]
            for g in range(1, groups):
                f = jnp.where(lane_group == g, product[g * half : (g + 1) * half, ls], f)
            rs = slice(side * half, (side + 1) * half)
            hs = slice(LEAD + side * half, LEAD + (side + 1) * half)
            out_ref[rs, cs] = (h_ref[hs, cs] + u_ref[rs, cs] * f).astype(BF16)

    @pl.loop(0, last_chunk)
    def _(k):
        @pl.when(has_behind)
        def _():
            part_copy(k).wait_recv()

        @pl.when(has_behind & (k < EARLY))
        def _():
            @pl.loop(0, here)
            def _(b):
                c = k * here + b
                cs = lanes_of(c)
                behind_ref[far : far + tap_count] = win_ref[:tap_count, cs].astype(F32)
                behind_ref[far + tap_count :] = before_ref[far:, cs]
                short_block(c, lambda _: behind_ref[...], tail, *share, halo_ref, 0, slice(None))
                taps = mr_taps_of(cs)
                z_ref[0:tail] = halo_ref[...] * told_ref[...]
                for first, size in pieces(tap_count):
                    win_ref[first : first + size, cs] = mr_product(taps, tail - tap_count - 8 + first, size)

        @pl.loop(0, here, step=STEP)
        def _(b):
            for slot in range(STEP):
                finish(k * here + b + slot, slot)

    @pl.loop(0, here)
    def _(b):
        @pl.when(has_behind)
        def _():
            last_copy(b).wait_recv()

        finish(last_chunk * here + b, 0)

    @pl.when(has_ahead)
    def _():
        near_copy().wait_send()
        tell_copy(0).wait_send()
        tell_copy(1).wait_send()

        @pl.loop(0, last_chunk)
        def _(k):
            part_copy(k).wait_send()

        @pl.loop(0, here)
        def _(b):
            last_copy(b).wait_send()

    @pl.when(is_relay)
    def _():
        @pl.loop(0, EARLY)
        def _(k):
            from_relay_copy(k).wait_send()

    @pl.when(is_side)
    def _():
        @pl.loop(EARLY, EARLY + SIDE)
        def _(k):
            from_side_copy(k).wait_send()


def on_device(axes, tokens, norm_gain, feat_taps, se_taps, mr_taps):
    rows, channels = tokens.shape
    tap_count, group_count = mr_taps.shape[1:]
    groups = LANES * group_count // channels
    blocks = channels // LANES
    spread = 2 * tap_count
    early_width = EARLY * channels // CHUNKS
    near_width = channels // SLICES
    operands = (tokens, norm_gain, feat_taps.transpose(0, 2, 3, 1, 4), se_taps.transpose(1, 0, 2), mr_taps)
    return pl.pallas_call(
        functools.partial(kernel, axes),
        out_shape=pltpu.VMEM((rows, channels), BF16),
        in_specs=[pl.BlockSpec(memory_space=pltpu.HBM)] * 5,
        out_specs=pl.BlockSpec(memory_space=pltpu.VMEM),
        scratch_shapes=[pltpu.VMEM(a.shape, a.dtype) for a in operands] + [
            pltpu.VMEM((tap_count, early_width), BF16),
            pltpu.VMEM((tap_count + rows, channels), BF16),
            pltpu.VMEM((LEAD + rows, channels), F32),
            pltpu.VMEM((rows, channels), F32),
            pltpu.VMEM((blocks, groups * rows // 2, spread), BF16),
            pltpu.VMEM((group_count, tap_count), F32),
            pltpu.VMEM((STEP, spread, 2 * LANES), BF16),
            pltpu.VMEM((LEAD + rows, LANES), F32),
            pltpu.VMEM((LEAD + rows, LANES), F32),
            pltpu.VMEM((LEAD + rows, LANES), F32),
            pltpu.VMEM((LEAD + rows, LANES), F32),
            pltpu.VMEM((LEAD + rows, LANES), F32),
            pltpu.VMEM((tap_count + LEAD, LANES), F32),
            pltpu.VMEM((tap_count + LEAD, LANES), F32),
            pltpu.VMEM((tap_count + LEAD, LANES), F32),
            pltpu.VMEM((LEAD, channels), F32),
            pltpu.VMEM((2, 8, LANES), F32),
            pltpu.VMEM((2, 8, LANES), F32),
            pltpu.VMEM((SLICES * NEAR, near_width), F32),
            pltpu.VMEM((SLICES * NEAR, near_width), BF16),
            pltpu.VMEM((SLICES * NEAR, near_width), BF16),
            pltpu.VMEM((tap_count, early_width), BF16),
            pltpu.SemaphoreType.DMA((6,)),
            pltpu.SemaphoreType.DMA((6,)),
            pltpu.SemaphoreType.DMA((CHUNKS,)),
            pltpu.SemaphoreType.DMA((CHUNKS,)),
            pltpu.SemaphoreType.DMA((EARLY,)),
            pltpu.SemaphoreType.DMA((EARLY,)),
            pltpu.VMEM((tap_count, SIDE * channels // CHUNKS), BF16),
            pltpu.SemaphoreType.DMA((SIDE,)),
            pltpu.SemaphoreType.DMA((SIDE,)),
            pltpu.SemaphoreType.DMA((blocks // CHUNKS,)),
            pltpu.SemaphoreType.DMA((blocks // CHUNKS,)),
        ],
        compiler_params=pltpu.CompilerParams(
            collective_id=0, has_side_effects=True, vmem_limit_bytes=58 * 1024 * 1024),
        name="pair",
    )(*operands)


def solution(mesh):
    axes = tuple(mesh.axis_names)
    placed = (P(axes, None), P(), P(), P(), P())
    return jax.shard_map(
        functools.partial(on_device, axes),
        mesh=mesh,
        in_specs=placed,
        out_specs=P(axes, None),
        check_vma=False,
    )
```

```python
import functools

import jax
import jax.numpy as jnp
from jax import lax
from jax.experimental import pallas as pl
from jax.experimental.pallas import tpu as pltpu
from jax.sharding import PartitionSpec as P

F32 = jnp.float32
BF16 = jnp.bfloat16
LANES = 128
CHUNKS = 16
EARLY = 4
MORE = 1
SIDE = 4
STEP = 4
LEAD = 16
NEAR = 9
SLICES = 16
MESH = pl.DeviceIdType.MESH


def lanes_of(c, width=LANES):
    return pl.ds(pl.multiple_of(c * width, width), width)


def row_scale(total, channels):
    mean = jnp.sum(total, axis=-1, keepdims=True) * (1.0 / channels)
    return jnp.broadcast_to(lax.rsqrt(mean + 1e-06), total.shape)


def square_sums(read, rows, blocks):
    def add(c, total):
        v = read(c).astype(F32)
        return total + v * v

    return lax.fori_loop(0, blocks, add, jnp.zeros((rows, LANES), F32))


def stream(z_ref, taps, first, rows):
    total = taps[0] * z_ref[8 + first : 8 + first + rows]
    for i in range(1, len(taps)):
        total = total + taps[i] * z_ref[8 + first - i : 8 + first - i + rows]
    return total


def feat_rows(feat_ref, o, gain, cs):
    streams, feat = feat_ref.shape[1:3]
    return [[feat_ref[0, j, i, o : o + 1, cs] * gain for i in range(feat)] for j in range(streams)]


def pieces(rows, most=48):
    return [(first, min(most, rows - first)) for first in range(0, rows, most)]


def short_block(c, read, rows, gain_ref, feat_ref, taps_ref, z_ref, w_ref, s_ref, h_ref, start, hs):
    cs = lanes_of(c)
    gain = gain_ref[0, 0:1, cs]
    taps = feat_rows(feat_ref, 0, gain, cs)
    short = [taps_ref[i, 0:1, cs] for i in range(taps_ref.shape[0])]
    z_ref[8 : 8 + rows] = read(c).astype(F32) * s_ref[:rows]
    for first, count in pieces(rows):
        u1 = stream(z_ref, taps[1], first, count)
        u2 = stream(z_ref, taps[2], first, count)
        w_ref[8 + first : 8 + first + count] = (u1 * u2).astype(BF16).astype(F32)
    for first, count in pieces(rows):
        f = stream(w_ref, short, first, count)
        u0 = stream(z_ref, taps[0], first, count)
        h_ref[start + first : start + first + count, hs] = u0 * f
    h = (h_ref[start : start + rows, hs] + read(c).astype(F32)).astype(BF16).astype(F32)
    h_ref[start : start + rows, hs] = h
    return h


def same_place(rows):
    return (lax.broadcasted_iota(jnp.int32, (rows, LANES), 0)
            == lax.broadcasted_iota(jnp.int32, (rows, LANES), 1))


def pack_rows(values_ref, start, rows, pack_ref):
    for r, (first, count) in enumerate(pieces(rows, LANES)):
        values = values_ref[start + first : start + first + count]
        pack_ref[r : r + 1] = jnp.sum(jnp.where(same_place(count), values, 0.0), axis=0, keepdims=True)


def unpack_rows(pack_ref, rows, values_ref):
    for r, (first, count) in enumerate(pieces(rows, LANES)):
        values = jnp.broadcast_to(pack_ref[r : r + 1], (count, LANES))
        column = jnp.sum(jnp.where(same_place(count), values, 0.0), axis=1, keepdims=True)
        values_ref[first : first + count] = jnp.broadcast_to(column, (count, LANES))


def kernel(axes, x_hbm, gain_hbm, feat_hbm, taps_hbm, mr_hbm, out_ref,
           x_ref, gain_ref, feat_ref, taps_ref, mr_ref,
           stage_ref, win_ref, h_ref, u_ref, table_ref, base_ref, rhs_ref, scale_ref, z_ref, w_ref,
           s_ref, sum_ref, halo_ref, behind_ref, told_ref, before_ref, give_ref, got_ref, near_ref, near_give_ref, near_got_ref, relay_ref,
           local_sems, lead_sems, send_sems, recv_sems, relay_send_sems, relay_recv_sems,
           side_ref, side_send_sems, side_recv_sems, last_send_sems, last_recv_sems):
    rows, channels = x_ref.shape
    tap_count, group_count = mr_ref.shape[1:]
    per_group = channels // group_count
    groups = LANES // per_group
    half = rows // 2
    blocks = channels // LANES
    part = channels // CHUNKS
    here = blocks // CHUNKS
    tail = tap_count + LEAD
    first_tail = rows - tail
    first_sent = rows - tap_count
    side_start = EARLY + MORE
    side_end = side_start + SIDE
    near_width = channels // SLICES
    far = LEAD - NEAR
    last_chunk = CHUNKS - 1
    outer, inner = axes
    inner_size = lax.axis_size(inner)
    count = lax.axis_size(outer) * inner_size
    me = lax.axis_index(outer) * inner_size + lax.axis_index(inner)
    behind, ahead = me - 1, me + 1
    has_behind, has_ahead = me > 0, me < count - 1
    sections, section = lax.axis_size(outer), lax.axis_index(outer)
    start_of, end_of = lax.axis_index(inner) == 0, lax.axis_index(inner) == inner_size - 1
    odd, even = section % 2 == 1, section % 2 == 0
    via_relay = end_of & odd & (section + 2 < sections)
    is_relay = end_of & odd & (section >= 3)
    is_side = start_of & even & (section + 3 < sections)
    past_relay = start_of & even & (section >= 2) & (section + 1 < sections)

    def place(index):
        return (index // inner_size, index % inner_size)

    barrier = pltpu.get_barrier_semaphore()

    @pl.when(has_behind)
    def _():
        pl.semaphore_signal(barrier, inc=1, device_id=place(behind), device_id_type=MESH)

    @pl.when(is_relay)
    def _():
        pl.semaphore_signal(barrier, inc=1, device_id=place(me - 2 * inner_size), device_id_type=MESH)

    @pl.when(is_side)
    def _():
        pl.semaphore_signal(barrier, inc=1, device_id=place(behind + 2 * inner_size), device_id_type=MESH)

    @pl.when(past_relay)
    def _():
        pl.semaphore_signal(barrier, inc=1, device_id=place(me - 2 * inner_size), device_id_type=MESH)
        pl.semaphore_signal(barrier, inc=1, device_id=place(behind + 2 * inner_size), device_id_type=MESH)

    loads = [pltpu.make_async_copy(src, dst, local_sems.at[i]) for i, (src, dst) in enumerate(
        [(x_hbm.at[pl.ds(rows - LEAD, LEAD)], x_ref.at[pl.ds(rows - LEAD, LEAD)]),
         (x_hbm.at[pl.ds(0, rows - LEAD)], x_ref.at[pl.ds(0, rows - LEAD)]), (gain_hbm, gain_ref), (feat_hbm, feat_ref), (taps_hbm, taps_ref), (mr_hbm, mr_ref)])]
    for load in loads:
        load.start()

    def to_device(index, src, dst, send_sem, recv_sem):
        return pltpu.make_async_remote_copy(
            src_ref=src, dst_ref=dst, send_sem=send_sem, recv_sem=recv_sem,
            device_id=place(index), device_id_type=MESH)

    to_ahead = functools.partial(to_device, ahead)

    def near_copy():
        return to_ahead(near_give_ref, near_got_ref, lead_sems.at[0], lead_sems.at[1])

    def tell_copy(o):
        return to_ahead(give_ref.at[o], got_ref.at[o], lead_sems.at[2 + 2 * o], lead_sems.at[3 + 2 * o])

    def part_copy(k):
        cs = lanes_of(k, part)
        return to_ahead(stage_ref.at[:, cs], win_ref.at[pl.ds(0, tap_count), cs],
                        send_sems.at[k], recv_sems.at[k])

    def to_relay_copy(k):
        cs = lanes_of(k, part)
        return to_device(me + 2 * inner_size, stage_ref.at[:, cs], relay_ref.at[:, cs], send_sems.at[k], relay_recv_sems.at[k])

    def from_relay_copy(k):
        cs = lanes_of(k, part)
        return to_device(me - 2 * inner_size + 1, relay_ref.at[:, cs], win_ref.at[pl.ds(0, tap_count), cs],
                         relay_send_sems.at[k], recv_sems.at[k])

    def side_columns(k):
        return lanes_of(k - side_start, part)

    def to_side_copy(k):
        return to_device(ahead - 2 * inner_size, stage_ref.at[:, lanes_of(k, part)],
                         side_ref.at[:, side_columns(k)], send_sems.at[k], side_recv_sems.at[k - side_start])

    def from_side_copy(k):
        return to_device(me + 2 * inner_size, side_ref.at[:, side_columns(k)],
                         win_ref.at[pl.ds(0, tap_count), lanes_of(k, part)],
                         side_send_sems.at[k - side_start], recv_sems.at[k])


    def last_copy(b):
        cs = lanes_of(last_chunk * here + b)
        return to_ahead(stage_ref.at[:, cs], win_ref.at[pl.ds(0, tap_count), cs],
                        last_send_sems.at[b], last_recv_sems.at[b])

    loads[0].wait()
    for i in range(SLICES):
        cs = slice(i * near_width, (i + 1) * near_width)
        near_ref[i * NEAR : (i + 1) * NEAR] = x_ref[rows - LEAD :, cs].astype(F32)[far:]
    near_give_ref[...] = near_ref[...].astype(BF16)
    greeted = [has_ahead, via_relay, via_relay, is_relay, is_side]
    pl.semaphore_wait(barrier, sum(g.astype(jnp.int32) for g in greeted))

    @pl.when(has_ahead)
    def _():
        near_copy().start()

    loads[1].wait()

    @pl.loop(0, EARLY)
    def _(k):
        @pl.loop(0, here)
        def _(b):
            cs = lanes_of(k * here + b)
            stage_ref[:, cs] = x_ref[first_tail:, cs].astype(F32)[far : far + tap_count].astype(BF16)

        @pl.when(has_ahead & jnp.logical_not(via_relay))
        def _():
            part_copy(k).start()

        @pl.when(via_relay)
        def _():
            to_relay_copy(k).start()

    z_ref[...] = jnp.zeros_like(z_ref)
    w_ref[...] = jnp.zeros_like(w_ref)
    give_ref[...] = jnp.zeros_like(give_ref)
    share = (gain_ref, feat_ref, taps_ref, z_ref, w_ref, s_ref)
    early_blocks = EARLY * here
    told_rows = len(pieces(tail, LANES))

    def mr_product(taps, first, size):
        return (stream(z_ref, taps[1], first, size) * stream(z_ref, taps[2], first, size)).astype(BF16)

    def with_first(row, product):
        first = lax.broadcasted_iota(jnp.int32, product.shape, 0) == 0
        return jnp.where(first, jnp.broadcast_to(row, product.shape), product.astype(F32)).astype(BF16)

    def mr_taps_of(cs):
        return feat_rows(feat_ref, 1, gain_ref[0, 1:2, cs], cs)

    read_tail = lambda c: x_ref[first_tail:, lanes_of(c)]
    s_ref[:tail] = row_scale(square_sums(read_tail, tail, blocks), channels)
    pack_rows(s_ref, 0, tail, give_ref.at[0])

    @pl.when(has_ahead)
    def _():
        tell_copy(0).start()

    for load in loads[2:]:
        load.wait()
    sum_ref[:tail] = jnp.zeros((tail, LANES), F32)
    start_tail = LEAD + first_tail

    @pl.loop(0, blocks)
    def _(c):
        h = short_block(c, read_tail, tail, *share, h_ref, start_tail, lanes_of(c))
        sum_ref[:tail] += h * h

    scale_ref[start_tail : start_tail + tail] = row_scale(sum_ref[:tail], channels)
    pack_rows(scale_ref, start_tail, tail, give_ref.at[1])
    for b in range(here):
        cs = slice((last_chunk * here + b) * LANES, (last_chunk * here + b + 1) * LANES)
        give_ref[1, told_rows + b : told_rows + b + 1] = h_ref[LEAD + rows - 2 : LEAD + rows - 1, cs]

    @pl.when(has_ahead)
    def _():
        tell_copy(1).start()

    def product_to_send(c):
        cs = lanes_of(c)
        taps = mr_taps_of(cs)
        n = tap_count + 8
        top = LEAD + first_sent - 8
        z_ref[0:n] = h_ref[top : top + n, cs] * scale_ref[top : top + n]
        for first, size in pieces(tap_count):
            product = mr_product(taps, first, size)
            win_ref[rows + first : rows + first + size, cs] = product
            if first == 0:
                product = with_first(h_ref[LEAD + rows - 2 : LEAD + rows - 1, cs], product)
            stage_ref[first : first + size, cs] = product

    @pl.loop(EARLY, last_chunk)
    def _(k):
        @pl.loop(0, here)
        def _(b):
            product_to_send(k * here + b)

        above = via_relay & (k < side_start)
        beside = via_relay & (k >= side_start) & (k < side_end)

        @pl.when(has_ahead & jnp.logical_not(above) & jnp.logical_not(beside))
        def _():
            part_copy(k).start()

        @pl.when(above)
        def _():
            to_relay_copy(k).start()

        @pl.when(beside)
        def _():
            to_side_copy(k).start()

    @pl.loop(0, here)
    def _(b):
        product_to_send(last_chunk * here + b)

        @pl.when(has_ahead)
        def _():
            last_copy(b).start()

    @pl.when(is_relay)
    def _():
        @pl.loop(0, EARLY)
        def _(k):
            to_relay_copy(k).wait_recv()
            from_relay_copy(k).start()

    at_tap = lax.broadcasted_iota(jnp.int32, (tap_count, tap_count), 0)
    at_lag = lax.broadcasted_iota(jnp.int32, (tap_count, tap_count), 1)
    flip = jnp.where((at_tap + at_lag == tap_count) | (at_tap + at_lag == 0), 1.0, 0.0).astype(BF16)
    past = (lax.broadcasted_iota(jnp.int32, (half, tap_count), 1)
            > lax.broadcasted_iota(jnp.int32, (half, tap_count), 0))
    base_ref[...] = lax.dot_general(mr_ref[0], flip, (((0,), (0,)), ((), ())),
                                    preferred_element_type=F32)
    rhs_ref[...] = jnp.zeros_like(rhs_ref)

    @pl.when(has_behind)
    def _():
        near_copy().wait_recv()

    @pl.when(jnp.logical_not(has_behind))
    def _():
        near_got_ref[...] = jnp.zeros_like(near_got_ref)
        got_ref[...] = jnp.zeros_like(got_ref)
        win_ref[:tap_count] = jnp.zeros((tap_count, channels), BF16)

    near_ref[...] = near_got_ref[...].astype(F32)
    for i in range(SLICES):
        cs = slice(i * near_width, (i + 1) * near_width)
        before_ref[:far, cs] = jnp.zeros((far, near_width), F32)
        before_ref[far:, cs] = near_ref[i * NEAR : (i + 1) * NEAR]

    head = LEAD + first_sent
    z_ref[0:8] = jnp.zeros((8, LANES), F32)
    read_head = lambda c: jnp.concatenate(
        [before_ref[:, lanes_of(c)], x_ref[:first_sent, lanes_of(c)].astype(F32)], axis=0)
    s_ref[:head] = row_scale(square_sums(read_head, head, blocks), channels)
    sum_ref[:head] = jnp.zeros((head, LANES), F32)

    @pl.loop(0, blocks)
    def _(c):
        h = short_block(c, read_head, head, *share, h_ref, 0, lanes_of(c))
        sum_ref[:head] += h * h

    scale_ref[:head] = row_scale(sum_ref[:head], channels)

    @pl.loop(0, blocks)
    def _(c):
        cs = lanes_of(c)
        taps = mr_taps_of(cs)
        z_ref[0 : rows + 8] = h_ref[LEAD - 8 :, cs] * scale_ref[LEAD - 8 :]

        def put(low, high):
            for first, size in pieces(high - low):
                first += low
                win_ref[tap_count + first : tap_count + first + size, cs] = mr_product(taps, first, size)

        put(LEAD, first_sent)

        @pl.when(c < early_blocks)
        def _():
            put(first_sent, rows)

        for first, size in pieces(rows - LEAD):
            first += LEAD
            u_ref[first : first + size, cs] = stream(z_ref, taps[0], first, size)

    @pl.when(is_relay)
    def _():
        @pl.loop(EARLY, side_start)
        def _(k):
            to_relay_copy(k).wait_recv()
            from_relay_copy(k).start()

    @pl.when(is_side)
    def _():
        @pl.loop(side_start, side_end)
        def _(k):
            to_side_copy(k).wait_recv()
            from_side_copy(k).start()

    @pl.loop(0, blocks)
    def _(c):
        lags = base_ref[pl.ds(pl.multiple_of(c * groups, groups), groups), :]
        for g in range(groups):
            row = jnp.broadcast_to(lags[g : g + 1], (half, tap_count))
            turned = pltpu.roll(row, 0, 1, stride=1, stride_axis=0)
            gs = slice(g * half, (g + 1) * half)
            table_ref[c, gs, :tap_count] = jnp.where(past, turned, 0.0).astype(BF16)
            table_ref[c, gs, tap_count:] = jnp.where(past, 0.0, turned).astype(BF16)

    lane_group = lax.broadcasted_iota(jnp.int32, (half, LANES), 1) // per_group
    reach = half + tap_count

    @pl.when(has_behind)
    def _():
        tell_copy(0).wait_recv()
        unpack_rows(got_ref.at[0], tail, s_ref)
        tell_copy(1).wait_recv()
        unpack_rows(got_ref.at[1], tail, told_ref)
        scale_ref[LEAD - 2 : LEAD - 1] = told_ref[tail - 2 : tail - 1]

    behind_ref[:far] = jnp.zeros((far, LANES), F32)

    def first_rows(c, before):
        cs = lanes_of(c)
        taps = mr_taps_of(cs)
        h_ref[LEAD - 2 : LEAD - 1, cs] = before
        top = LEAD + 8
        z_ref[0:top] = h_ref[LEAD - 8 : LEAD + LEAD, cs] * scale_ref[LEAD - 8 : LEAD + LEAD]
        win_ref[tap_count : tap_count + LEAD, cs] = mr_product(taps, 0, LEAD)
        u_ref[0:LEAD, cs] = stream(z_ref, taps[0], 0, LEAD)

    def finish(c, slot):
        cs = lanes_of(c)
        rhs_ref[slot, :reach, :LANES] = win_ref[:reach, cs]
        rhs_ref[slot, :reach, LANES:] = win_ref[half : half + reach, cs]
        product = jnp.dot(table_ref[c], rhs_ref[slot], preferred_element_type=F32)
        for side in range(2):
            ls = slice(side * LANES, (side + 1) * LANES)
            f = product[0:half, ls]
            for g in range(1, groups):
                f = jnp.where(lane_group == g, product[g * half : (g + 1) * half, ls], f)
            rs = slice(side * half, (side + 1) * half)
            hs = slice(LEAD + side * half, LEAD + (side + 1) * half)
            out_ref[rs, cs] = (h_ref[hs, cs] + u_ref[rs, cs] * f).astype(BF16)

    @pl.loop(0, last_chunk)
    def _(k):
        @pl.when(has_behind)
        def _():
            part_copy(k).wait_recv()

        @pl.when(has_behind & (k < EARLY))
        def _():
            @pl.loop(0, here)
            def _(b):
                c = k * here + b
                cs = lanes_of(c)
                behind_ref[far : far + tap_count] = win_ref[:tap_count, cs].astype(F32)
                behind_ref[far + tap_count :] = before_ref[far:, cs]
                short_block(c, lambda _: behind_ref[...], tail, *share, halo_ref, 0, slice(None))
                taps = mr_taps_of(cs)
                z_ref[0:tail] = halo_ref[...] * told_ref[...]
                for first, size in pieces(tap_count):
                    product = mr_product(taps, tail - tap_count - 8 + first, size)
                    if first == 0:
                        product = with_first(halo_ref[tail - 2 : tail - 1], product)
                    win_ref[first : first + size, cs] = product

        @pl.loop(0, here, step=STEP)
        def _(b):
            for slot in range(STEP):
                c = k * here + b + slot
                first_rows(c, win_ref[:LEAD, lanes_of(c)].astype(F32)[0:1])
            for slot in range(STEP):
                finish(k * here + b + slot, slot)

    for b in range(here):
        first_rows(last_chunk * here + b, got_ref[1, told_rows + b : told_rows + b + 1])

    @pl.loop(0, here)
    def _(b):
        @pl.when(has_behind)
        def _():
            last_copy(b).wait_recv()

        finish(last_chunk * here + b, 0)

    @pl.when(has_ahead)
    def _():
        near_copy().wait_send()
        tell_copy(0).wait_send()
        tell_copy(1).wait_send()

        @pl.loop(0, last_chunk)
        def _(k):
            part_copy(k).wait_send()

        @pl.loop(0, here)
        def _(b):
            last_copy(b).wait_send()

    @pl.when(is_relay)
    def _():
        @pl.loop(0, side_start)
        def _(k):
            from_relay_copy(k).wait_send()

    @pl.when(is_side)
    def _():
        @pl.loop(side_start, side_end)
        def _(k):
            from_side_copy(k).wait_send()


def on_device(axes, tokens, norm_gain, feat_taps, se_taps, mr_taps):
    rows, channels = tokens.shape
    tap_count, group_count = mr_taps.shape[1:]
    groups = LANES * group_count // channels
    blocks = channels // LANES
    spread = 2 * tap_count
    near_width = channels // SLICES
    operands = (tokens, norm_gain, feat_taps.transpose(0, 2, 3, 1, 4), se_taps.transpose(1, 0, 2), mr_taps)
    return pl.pallas_call(
        functools.partial(kernel, axes),
        out_shape=pltpu.VMEM((rows, channels), BF16),
        in_specs=[pl.BlockSpec(memory_space=pltpu.HBM)] * 5,
        out_specs=pl.BlockSpec(memory_space=pltpu.VMEM),
        scratch_shapes=[pltpu.VMEM(a.shape, a.dtype) for a in operands] + [
            pltpu.VMEM((tap_count, channels), BF16),
            pltpu.VMEM((tap_count + rows, channels), BF16),
            pltpu.VMEM((LEAD + rows, channels), F32),
            pltpu.VMEM((rows, channels), F32),
            pltpu.VMEM((blocks, groups * rows // 2, spread), BF16),
            pltpu.VMEM((group_count, tap_count), F32),
            pltpu.VMEM((STEP, spread, 2 * LANES), BF16),
            pltpu.VMEM((LEAD + rows, LANES), F32),
            pltpu.VMEM((LEAD + rows, LANES), F32),
            pltpu.VMEM((LEAD + rows, LANES), F32),
            pltpu.VMEM((LEAD + rows, LANES), F32),
            pltpu.VMEM((LEAD + rows, LANES), F32),
            pltpu.VMEM((tap_count + LEAD, LANES), F32),
            pltpu.VMEM((tap_count + LEAD, LANES), F32),
            pltpu.VMEM((tap_count + LEAD, LANES), F32),
            pltpu.VMEM((LEAD, channels), F32),
            pltpu.VMEM((2, 8, LANES), F32),
            pltpu.VMEM((2, 8, LANES), F32),
            pltpu.VMEM((SLICES * NEAR, near_width), F32),
            pltpu.VMEM((SLICES * NEAR, near_width), BF16),
            pltpu.VMEM((SLICES * NEAR, near_width), BF16),
            pltpu.VMEM((tap_count, (EARLY + MORE) * channels // CHUNKS), BF16),
            pltpu.SemaphoreType.DMA((6,)),
            pltpu.SemaphoreType.DMA((6,)),
            pltpu.SemaphoreType.DMA((CHUNKS,)),
            pltpu.SemaphoreType.DMA((CHUNKS,)),
            pltpu.SemaphoreType.DMA((EARLY + MORE,)),
            pltpu.SemaphoreType.DMA((EARLY + MORE,)),
            pltpu.VMEM((tap_count, SIDE * channels // CHUNKS), BF16),
            pltpu.SemaphoreType.DMA((SIDE,)),
            pltpu.SemaphoreType.DMA((SIDE,)),
            pltpu.SemaphoreType.DMA((blocks // CHUNKS,)),
            pltpu.SemaphoreType.DMA((blocks // CHUNKS,)),
        ],
        compiler_params=pltpu.CompilerParams(
            collective_id=0, has_side_effects=True, vmem_limit_bytes=58 * 1024 * 1024),
        name="pair",
    )(*operands)


def solution(mesh):
    axes = tuple(mesh.axis_names)
    placed = (P(axes, None), P(), P(), P(), P())
    return jax.shard_map(
        functools.partial(on_device, axes),
        mesh=mesh,
        in_specs=placed,
        out_specs=P(axes, None),
        check_vma=False,
    )
```

```python
import functools

import jax
import jax.numpy as jnp
from jax import lax
from jax.experimental import pallas as pl
from jax.experimental.pallas import tpu as pltpu
from jax.sharding import PartitionSpec as P

F32 = jnp.float32
BF16 = jnp.bfloat16
LANES = 128
CHUNKS = 16
EARLY = 5
MORE = 0
SIDE = 4
STEP = 4
LEAD = 16
NEAR = 9
SLICES = 16
MESH = pl.DeviceIdType.MESH


def lanes_of(c, width=LANES):
    return pl.ds(pl.multiple_of(c * width, width), width)


def row_scale(total, channels):
    mean = jnp.sum(total, axis=-1, keepdims=True) * (1.0 / channels)
    return jnp.broadcast_to(lax.rsqrt(mean + 1e-06), total.shape)


def square_sums(read, rows, blocks):
    def add(c, total):
        v = read(c).astype(F32)
        return total + v * v

    return lax.fori_loop(0, blocks, add, jnp.zeros((rows, LANES), F32))


def stream(z_ref, taps, first, rows):
    total = taps[0] * z_ref[8 + first : 8 + first + rows]
    for i in range(1, len(taps)):
        total = total + taps[i] * z_ref[8 + first - i : 8 + first - i + rows]
    return total


def feat_rows(feat_ref, o, gain, cs):
    streams, feat = feat_ref.shape[1:3]
    return [[feat_ref[0, j, i, o : o + 1, cs] * gain for i in range(feat)] for j in range(streams)]


def pieces(rows, most=48):
    return [(first, min(most, rows - first)) for first in range(0, rows, most)]


def short_block(c, read, rows, gain_ref, feat_ref, taps_ref, z_ref, w_ref, s_ref, h_ref, start, hs):
    cs = lanes_of(c)
    gain = gain_ref[0, 0:1, cs]
    taps = feat_rows(feat_ref, 0, gain, cs)
    short = [taps_ref[i, 0:1, cs] for i in range(taps_ref.shape[0])]
    z_ref[8 : 8 + rows] = read(c).astype(F32) * s_ref[:rows]
    for first, count in pieces(rows):
        u1 = stream(z_ref, taps[1], first, count)
        u2 = stream(z_ref, taps[2], first, count)
        w_ref[8 + first : 8 + first + count] = (u1 * u2).astype(BF16).astype(F32)
    for first, count in pieces(rows):
        f = stream(w_ref, short, first, count)
        u0 = stream(z_ref, taps[0], first, count)
        h_ref[start + first : start + first + count, hs] = u0 * f
    h = (h_ref[start : start + rows, hs] + read(c).astype(F32)).astype(BF16).astype(F32)
    h_ref[start : start + rows, hs] = h
    return h


def same_place(rows):
    return (lax.broadcasted_iota(jnp.int32, (rows, LANES), 0)
            == lax.broadcasted_iota(jnp.int32, (rows, LANES), 1))


def pack_rows(values_ref, start, rows, pack_ref):
    for r, (first, count) in enumerate(pieces(rows, LANES)):
        values = values_ref[start + first : start + first + count]
        pack_ref[r : r + 1] = jnp.sum(jnp.where(same_place(count), values, 0.0), axis=0, keepdims=True)


def unpack_rows(pack_ref, rows, values_ref):
    for r, (first, count) in enumerate(pieces(rows, LANES)):
        values = jnp.broadcast_to(pack_ref[r : r + 1], (count, LANES))
        column = jnp.sum(jnp.where(same_place(count), values, 0.0), axis=1, keepdims=True)
        values_ref[first : first + count] = jnp.broadcast_to(column, (count, LANES))


def combine(product, h, u, groups, half, write):
    lane_group = lax.broadcasted_iota(jnp.int32, (half, LANES), 1) // (LANES // groups)
    for side in range(2):
        ls = slice(side * LANES, (side + 1) * LANES)
        f = product[0:half, ls]
        for g in range(1, groups):
            f = jnp.where(lane_group == g, product[g * half : (g + 1) * half, ls], f)
        write(slice(side * half, (side + 1) * half), (h(side) + u(side) * f).astype(BF16))


def write_out(groups, main_ref, rhs_ref, table_ref, h_ref, u_ref, out_ref, end_ref, sems):
    rows, channels = main_ref.shape
    half = rows // 2
    width = channels - LANES
    main = pltpu.make_async_copy(main_ref.at[:, pl.ds(0, width)], out_ref.at[:, pl.ds(0, width)], sems.at[0])
    main.start()

    def write(rs, values):
        end_ref[rs] = values

    part = lambda ref: lambda side: ref[side * half : (side + 1) * half]
    product = jnp.dot(table_ref[...], rhs_ref[...], preferred_element_type=F32)
    combine(product, part(h_ref), part(u_ref), groups, half, write)
    end = pltpu.make_async_copy(end_ref, out_ref.at[:, pl.ds(width, LANES)], sems.at[1])
    end.start()
    main.wait()
    end.wait()


def kernel(axes, x_hbm, gain_hbm, feat_hbm, taps_hbm, mr_hbm, out_ref, end_rhs_ref, end_table_ref, end_h_ref, end_u_ref,
           x_ref, gain_ref, feat_ref, taps_ref, mr_ref,
           stage_ref, win_ref, h_ref, u_ref, table_ref, base_ref, rhs_ref, scale_ref, z_ref, w_ref,
           s_ref, sum_ref, halo_ref, behind_ref, told_ref, before_ref, give_ref, got_ref, near_ref, near_give_ref, near_got_ref, relay_ref,
           local_sems, lead_sems, send_sems, recv_sems, relay_send_sems, relay_recv_sems,
           side_ref, side_send_sems, side_recv_sems, last_send_sems, last_recv_sems):
    rows, channels = x_ref.shape
    tap_count, group_count = mr_ref.shape[1:]
    per_group = channels // group_count
    groups = LANES // per_group
    half = rows // 2
    blocks = channels // LANES
    part = channels // CHUNKS
    here = blocks // CHUNKS
    tail = tap_count + LEAD
    first_tail = rows - tail
    first_sent = rows - tap_count
    side_start = EARLY + MORE
    side_end = side_start + SIDE
    near_width = channels // SLICES
    far = LEAD - NEAR
    last_chunk = CHUNKS - 1
    outer, inner = axes
    inner_size = lax.axis_size(inner)
    count = lax.axis_size(outer) * inner_size
    me = lax.axis_index(outer) * inner_size + lax.axis_index(inner)
    behind, ahead = me - 1, me + 1
    has_behind, has_ahead = me > 0, me < count - 1
    sections, section = lax.axis_size(outer), lax.axis_index(outer)
    start_of, end_of = lax.axis_index(inner) == 0, lax.axis_index(inner) == inner_size - 1
    odd, even = section % 2 == 1, section % 2 == 0
    via_relay = end_of & odd & (section + 2 < sections)
    is_relay = end_of & odd & (section >= 3)
    is_side = start_of & even & (section + 3 < sections)
    past_relay = start_of & even & (section >= 2) & (section + 1 < sections)

    def place(index):
        return (index // inner_size, index % inner_size)

    barrier = pltpu.get_barrier_semaphore()

    @pl.when(has_behind)
    def _():
        pl.semaphore_signal(barrier, inc=1, device_id=place(behind), device_id_type=MESH)

    @pl.when(is_relay)
    def _():
        pl.semaphore_signal(barrier, inc=1, device_id=place(me - 2 * inner_size), device_id_type=MESH)

    @pl.when(is_side)
    def _():
        pl.semaphore_signal(barrier, inc=1, device_id=place(behind + 2 * inner_size), device_id_type=MESH)

    @pl.when(past_relay)
    def _():
        pl.semaphore_signal(barrier, inc=1, device_id=place(me - 2 * inner_size), device_id_type=MESH)
        pl.semaphore_signal(barrier, inc=1, device_id=place(behind + 2 * inner_size), device_id_type=MESH)

    loads = [pltpu.make_async_copy(src, dst, local_sems.at[i]) for i, (src, dst) in enumerate(
        [(x_hbm.at[pl.ds(rows - LEAD, LEAD)], x_ref.at[pl.ds(rows - LEAD, LEAD)]),
         (x_hbm.at[pl.ds(0, rows - LEAD)], x_ref.at[pl.ds(0, rows - LEAD)]), (gain_hbm, gain_ref), (feat_hbm, feat_ref), (taps_hbm, taps_ref), (mr_hbm, mr_ref)])]
    for load in loads:
        load.start()

    def to_device(index, src, dst, send_sem, recv_sem):
        return pltpu.make_async_remote_copy(
            src_ref=src, dst_ref=dst, send_sem=send_sem, recv_sem=recv_sem,
            device_id=place(index), device_id_type=MESH)

    to_ahead = functools.partial(to_device, ahead)

    def near_copy():
        return to_ahead(near_give_ref, near_got_ref, lead_sems.at[0], lead_sems.at[1])

    def tell_copy(o):
        return to_ahead(give_ref.at[o], got_ref.at[o], lead_sems.at[2 + 2 * o], lead_sems.at[3 + 2 * o])

    def part_copy(k):
        cs = lanes_of(k, part)
        return to_ahead(stage_ref.at[:, cs], win_ref.at[pl.ds(0, tap_count), cs],
                        send_sems.at[k], recv_sems.at[k])

    def to_relay_copy(k):
        cs = lanes_of(k, part)
        return to_device(me + 2 * inner_size, stage_ref.at[:, cs], relay_ref.at[:, cs], send_sems.at[k], relay_recv_sems.at[k])

    def from_relay_copy(k):
        cs = lanes_of(k, part)
        return to_device(me - 2 * inner_size + 1, relay_ref.at[:, cs], win_ref.at[pl.ds(0, tap_count), cs],
                         relay_send_sems.at[k], recv_sems.at[k])

    def side_columns(k):
        return lanes_of(k - side_start, part)

    def to_side_copy(k):
        return to_device(ahead - 2 * inner_size, stage_ref.at[:, lanes_of(k, part)],
                         side_ref.at[:, side_columns(k)], send_sems.at[k], side_recv_sems.at[k - side_start])

    def from_side_copy(k):
        return to_device(me + 2 * inner_size, side_ref.at[:, side_columns(k)],
                         win_ref.at[pl.ds(0, tap_count), lanes_of(k, part)],
                         side_send_sems.at[k - side_start], recv_sems.at[k])


    def last_copy(b):
        cs = lanes_of(last_chunk * here + b)
        return to_ahead(stage_ref.at[:, cs], win_ref.at[pl.ds(0, tap_count), cs],
                        last_send_sems.at[b], last_recv_sems.at[b])

    loads[0].wait()
    for i in range(SLICES):
        cs = slice(i * near_width, (i + 1) * near_width)
        near_ref[i * NEAR : (i + 1) * NEAR] = x_ref[rows - LEAD :, cs].astype(F32)[far:]
    near_give_ref[...] = near_ref[...].astype(BF16)
    greeted = [has_ahead, via_relay, via_relay, is_relay, is_side]
    pl.semaphore_wait(barrier, sum(g.astype(jnp.int32) for g in greeted))

    @pl.when(has_ahead)
    def _():
        near_copy().start()

    loads[1].wait()

    @pl.loop(0, EARLY)
    def _(k):
        @pl.loop(0, here)
        def _(b):
            cs = lanes_of(k * here + b)
            stage_ref[:, cs] = x_ref[first_tail:, cs].astype(F32)[far : far + tap_count].astype(BF16)

        @pl.when(has_ahead & jnp.logical_not(via_relay))
        def _():
            part_copy(k).start()

        @pl.when(via_relay)
        def _():
            to_relay_copy(k).start()

    z_ref[...] = jnp.zeros_like(z_ref)
    w_ref[...] = jnp.zeros_like(w_ref)
    give_ref[...] = jnp.zeros_like(give_ref)
    share = (gain_ref, feat_ref, taps_ref, z_ref, w_ref, s_ref)
    early_blocks = EARLY * here
    told_rows = len(pieces(tail, LANES))

    def mr_product(taps, first, size):
        return (stream(z_ref, taps[1], first, size) * stream(z_ref, taps[2], first, size)).astype(BF16)

    def with_first(row, product):
        first = lax.broadcasted_iota(jnp.int32, product.shape, 0) == 0
        return jnp.where(first, jnp.broadcast_to(row, product.shape), product.astype(F32)).astype(BF16)

    def mr_taps_of(cs):
        return feat_rows(feat_ref, 1, gain_ref[0, 1:2, cs], cs)

    read_tail = lambda c: x_ref[first_tail:, lanes_of(c)]
    s_ref[:tail] = row_scale(square_sums(read_tail, tail, blocks), channels)
    pack_rows(s_ref, 0, tail, give_ref.at[0])

    @pl.when(has_ahead)
    def _():
        tell_copy(0).start()

    for load in loads[2:]:
        load.wait()
    sum_ref[:tail] = jnp.zeros((tail, LANES), F32)
    start_tail = LEAD + first_tail

    @pl.loop(0, blocks)
    def _(c):
        h = short_block(c, read_tail, tail, *share, h_ref, start_tail, lanes_of(c))
        sum_ref[:tail] += h * h

    scale_ref[start_tail : start_tail + tail] = row_scale(sum_ref[:tail], channels)
    pack_rows(scale_ref, start_tail, tail, give_ref.at[1])
    for b in range(here):
        cs = slice((last_chunk * here + b) * LANES, (last_chunk * here + b + 1) * LANES)
        give_ref[1, told_rows + b : told_rows + b + 1] = h_ref[LEAD + rows - 2 : LEAD + rows - 1, cs]

    @pl.when(has_ahead)
    def _():
        tell_copy(1).start()

    def product_to_send(c):
        cs = lanes_of(c)
        taps = mr_taps_of(cs)
        n = tap_count + 8
        top = LEAD + first_sent - 8
        z_ref[0:n] = h_ref[top : top + n, cs] * scale_ref[top : top + n]
        for first, size in pieces(tap_count):
            product = mr_product(taps, first, size)
            win_ref[rows + first : rows + first + size, cs] = product
            if first == 0:
                product = with_first(h_ref[LEAD + rows - 2 : LEAD + rows - 1, cs], product)
            stage_ref[first : first + size, cs] = product

    @pl.loop(EARLY, last_chunk)
    def _(k):
        @pl.loop(0, here)
        def _(b):
            product_to_send(k * here + b)

        above = via_relay & (k < side_start)
        beside = via_relay & (k >= side_start) & (k < side_end)

        @pl.when(has_ahead & jnp.logical_not(above) & jnp.logical_not(beside))
        def _():
            part_copy(k).start()

        @pl.when(above)
        def _():
            to_relay_copy(k).start()

        @pl.when(beside)
        def _():
            to_side_copy(k).start()

    @pl.loop(0, here)
    def _(b):
        product_to_send(last_chunk * here + b)

        @pl.when(has_ahead)
        def _():
            last_copy(b).start()

    @pl.when(is_relay)
    def _():
        @pl.loop(0, EARLY)
        def _(k):
            to_relay_copy(k).wait_recv()
            from_relay_copy(k).start()

    at_tap = lax.broadcasted_iota(jnp.int32, (tap_count, tap_count), 0)
    at_lag = lax.broadcasted_iota(jnp.int32, (tap_count, tap_count), 1)
    flip = jnp.where((at_tap + at_lag == tap_count) | (at_tap + at_lag == 0), 1.0, 0.0).astype(BF16)
    past = (lax.broadcasted_iota(jnp.int32, (half, tap_count), 1)
            > lax.broadcasted_iota(jnp.int32, (half, tap_count), 0))
    base_ref[...] = lax.dot_general(mr_ref[0], flip, (((0,), (0,)), ((), ())),
                                    preferred_element_type=F32)
    rhs_ref[...] = jnp.zeros_like(rhs_ref)

    @pl.when(has_behind)
    def _():
        near_copy().wait_recv()

    @pl.when(jnp.logical_not(has_behind))
    def _():
        near_got_ref[...] = jnp.zeros_like(near_got_ref)
        got_ref[...] = jnp.zeros_like(got_ref)
        win_ref[:tap_count] = jnp.zeros((tap_count, channels), BF16)

    near_ref[...] = near_got_ref[...].astype(F32)
    for i in range(SLICES):
        cs = slice(i * near_width, (i + 1) * near_width)
        before_ref[:far, cs] = jnp.zeros((far, near_width), F32)
        before_ref[far:, cs] = near_ref[i * NEAR : (i + 1) * NEAR]

    head = LEAD + first_sent
    z_ref[0:8] = jnp.zeros((8, LANES), F32)
    read_head = lambda c: jnp.concatenate(
        [before_ref[:, lanes_of(c)], x_ref[:first_sent, lanes_of(c)].astype(F32)], axis=0)
    s_ref[:head] = row_scale(square_sums(read_head, head, blocks), channels)
    sum_ref[:head] = jnp.zeros((head, LANES), F32)

    @pl.loop(0, blocks)
    def _(c):
        h = short_block(c, read_head, head, *share, h_ref, 0, lanes_of(c))
        sum_ref[:head] += h * h

    scale_ref[:head] = row_scale(sum_ref[:head], channels)

    @pl.loop(0, blocks)
    def _(c):
        cs = lanes_of(c)
        taps = mr_taps_of(cs)
        z_ref[0 : rows + 8] = h_ref[LEAD - 8 :, cs] * scale_ref[LEAD - 8 :]

        def put(low, high):
            for first, size in pieces(high - low):
                first += low
                win_ref[tap_count + first : tap_count + first + size, cs] = mr_product(taps, first, size)

        put(LEAD, first_sent)

        @pl.when(c < early_blocks)
        def _():
            put(first_sent, rows)

        for first, size in pieces(rows - LEAD):
            first += LEAD
            u_ref[first : first + size, cs] = stream(z_ref, taps[0], first, size)

    @pl.when(is_relay)
    def _():
        @pl.loop(EARLY, side_start)
        def _(k):
            to_relay_copy(k).wait_recv()
            from_relay_copy(k).start()

    @pl.when(is_side)
    def _():
        @pl.loop(side_start, side_end)
        def _(k):
            to_side_copy(k).wait_recv()
            from_side_copy(k).start()

    @pl.loop(0, blocks)
    def _(c):
        lags = base_ref[pl.ds(pl.multiple_of(c * groups, groups), groups), :]
        for g in range(groups):
            row = jnp.broadcast_to(lags[g : g + 1], (half, tap_count))
            turned = pltpu.roll(row, 0, 1, stride=1, stride_axis=0)
            gs = slice(g * half, (g + 1) * half)
            table_ref[c, gs, :tap_count] = jnp.where(past, turned, 0.0).astype(BF16)
            table_ref[c, gs, tap_count:] = jnp.where(past, 0.0, turned).astype(BF16)

    reach = half + tap_count

    @pl.when(has_behind)
    def _():
        tell_copy(0).wait_recv()
        unpack_rows(got_ref.at[0], tail, s_ref)
        tell_copy(1).wait_recv()
        unpack_rows(got_ref.at[1], tail, told_ref)
        scale_ref[LEAD - 2 : LEAD - 1] = told_ref[tail - 2 : tail - 1]

    behind_ref[:far] = jnp.zeros((far, LANES), F32)

    def first_rows(c, before):
        cs = lanes_of(c)
        taps = mr_taps_of(cs)
        h_ref[LEAD - 2 : LEAD - 1, cs] = before
        top = LEAD + 8
        z_ref[0:top] = h_ref[LEAD - 8 : LEAD + LEAD, cs] * scale_ref[LEAD - 8 : LEAD + LEAD]
        win_ref[tap_count : tap_count + LEAD, cs] = mr_product(taps, 0, LEAD)
        u_ref[0:LEAD, cs] = stream(z_ref, taps[0], 0, LEAD)

    shared = tap_count - half

    def place_own(c, slot):
        cs = lanes_of(c)
        rhs_ref[slot, tap_count:reach, :LANES] = win_ref[tap_count:reach, cs]
        rhs_ref[slot, shared:reach, LANES:] = win_ref[tap_count : half + reach, cs]

    def place_halo(c, slot):
        cs = lanes_of(c)
        rhs_ref[slot, :tap_count, :LANES] = win_ref[:tap_count, cs]
        rhs_ref[slot, :shared, LANES:] = win_ref[half:tap_count, cs]

    def finish(c, slot):
        cs = lanes_of(c)
        place_halo(c, slot)
        product = jnp.dot(table_ref[c], rhs_ref[slot], preferred_element_type=F32)

        def write(rs, values):
            out_ref[rs, cs] = values

        combine(product, lambda side: h_ref[LEAD + side * half : LEAD + (side + 1) * half, cs],
                lambda side: u_ref[side * half : (side + 1) * half, cs], groups, half, write)

    @pl.loop(0, last_chunk)
    def _(k):
        @pl.when(has_behind)
        def _():
            part_copy(k).wait_recv()

        @pl.when(has_behind & (k < EARLY))
        def _():
            @pl.loop(0, here)
            def _(b):
                c = k * here + b
                cs = lanes_of(c)
                behind_ref[far : far + tap_count] = win_ref[:tap_count, cs].astype(F32)
                behind_ref[far + tap_count :] = before_ref[far:, cs]
                short_block(c, lambda _: behind_ref[...], tail, *share, halo_ref, 0, slice(None))
                taps = mr_taps_of(cs)
                z_ref[0:tail] = halo_ref[...] * told_ref[...]
                for first, size in pieces(tap_count):
                    product = mr_product(taps, tail - tap_count - 8 + first, size)
                    if first == 0:
                        product = with_first(halo_ref[tail - 2 : tail - 1], product)
                    win_ref[first : first + size, cs] = product

        @pl.loop(0, here, step=STEP)
        def _(b):
            for slot in range(STEP):
                c = k * here + b + slot
                first_rows(c, win_ref[:LEAD, lanes_of(c)].astype(F32)[0:1])
            for slot in range(STEP):
                place_own(k * here + b + slot, slot)
                finish(k * here + b + slot, slot)

    for b in range(here):
        first_rows(last_chunk * here + b, got_ref[1, told_rows + b : told_rows + b + 1])
        place_own(last_chunk * here + b, b)

    end_rhs_ref[...] = rhs_ref[here - 1]
    end_table_ref[...] = table_ref[blocks - 1]
    end_h_ref[...] = h_ref[LEAD:, channels - LANES :]
    end_u_ref[...] = u_ref[:, channels - LANES :]

    @pl.loop(0, here - 1)
    def _(b):
        @pl.when(has_behind)
        def _():
            last_copy(b).wait_recv()

        finish(last_chunk * here + b, b)

    @pl.when(has_behind)
    def _():
        last_copy(here - 1).wait_recv()

    end_rhs_ref[:tap_count, :LANES] = win_ref[:tap_count, channels - LANES :]
    end_rhs_ref[:shared, LANES:] = win_ref[half:tap_count, channels - LANES :]

    @pl.when(has_ahead)
    def _():
        near_copy().wait_send()
        tell_copy(0).wait_send()
        tell_copy(1).wait_send()

        @pl.loop(0, last_chunk)
        def _(k):
            part_copy(k).wait_send()

        @pl.loop(0, here)
        def _(b):
            last_copy(b).wait_send()

    @pl.when(is_relay)
    def _():
        @pl.loop(0, side_start)
        def _(k):
            from_relay_copy(k).wait_send()

    @pl.when(is_side)
    def _():
        @pl.loop(side_start, side_end)
        def _(k):
            from_side_copy(k).wait_send()


def on_device(axes, tokens, norm_gain, feat_taps, se_taps, mr_taps):
    rows, channels = tokens.shape
    tap_count, group_count = mr_taps.shape[1:]
    groups = LANES * group_count // channels
    blocks = channels // LANES
    spread = 2 * tap_count
    here = blocks // CHUNKS
    near_width = channels // SLICES
    operands = (tokens, norm_gain, feat_taps.transpose(0, 2, 3, 1, 4), se_taps.transpose(1, 0, 2), mr_taps)
    results = pl.pallas_call(
        functools.partial(kernel, axes),
        out_shape=(
            pltpu.VMEM((rows, channels), BF16),
            pltpu.VMEM((spread, 2 * LANES), BF16),
            pltpu.VMEM((groups * rows // 2, spread), BF16),
            pltpu.VMEM((rows, LANES), F32),
            pltpu.VMEM((rows, LANES), F32),
        ),
        in_specs=[pl.BlockSpec(memory_space=pltpu.HBM)] * 5,
        out_specs=(pl.BlockSpec(memory_space=pltpu.VMEM),) * 5,
        scratch_shapes=[pltpu.VMEM(a.shape, a.dtype) for a in operands] + [
            pltpu.VMEM((tap_count, channels), BF16),
            pltpu.VMEM((tap_count + rows, channels), BF16),
            pltpu.VMEM((LEAD + rows, channels), F32),
            pltpu.VMEM((rows, channels), F32),
            pltpu.VMEM((blocks, groups * rows // 2, spread), BF16),
            pltpu.VMEM((group_count, tap_count), F32),
            pltpu.VMEM((max(STEP, here), spread, 2 * LANES), BF16),
            pltpu.VMEM((LEAD + rows, LANES), F32),
            pltpu.VMEM((LEAD + rows, LANES), F32),
            pltpu.VMEM((LEAD + rows, LANES), F32),
            pltpu.VMEM((LEAD + rows, LANES), F32),
            pltpu.VMEM((LEAD + rows, LANES), F32),
            pltpu.VMEM((tap_count + LEAD, LANES), F32),
            pltpu.VMEM((tap_count + LEAD, LANES), F32),
            pltpu.VMEM((tap_count + LEAD, LANES), F32),
            pltpu.VMEM((LEAD, channels), F32),
            pltpu.VMEM((2, 8, LANES), F32),
            pltpu.VMEM((2, 8, LANES), F32),
            pltpu.VMEM((SLICES * NEAR, near_width), F32),
            pltpu.VMEM((SLICES * NEAR, near_width), BF16),
            pltpu.VMEM((SLICES * NEAR, near_width), BF16),
            pltpu.VMEM((tap_count, (EARLY + MORE) * channels // CHUNKS), BF16),
            pltpu.SemaphoreType.DMA((6,)),
            pltpu.SemaphoreType.DMA((6,)),
            pltpu.SemaphoreType.DMA((CHUNKS,)),
            pltpu.SemaphoreType.DMA((CHUNKS,)),
            pltpu.SemaphoreType.DMA((EARLY + MORE,)),
            pltpu.SemaphoreType.DMA((EARLY + MORE,)),
            pltpu.VMEM((tap_count, SIDE * channels // CHUNKS), BF16),
            pltpu.SemaphoreType.DMA((SIDE,)),
            pltpu.SemaphoreType.DMA((SIDE,)),
            pltpu.SemaphoreType.DMA((blocks // CHUNKS,)),
            pltpu.SemaphoreType.DMA((blocks // CHUNKS,)),
        ],
        compiler_params=pltpu.CompilerParams(
            collective_id=0, has_side_effects=True, vmem_limit_bytes=57 * 1024 * 1024),
        name="pair",
    )(*operands)
    return pl.pallas_call(
        functools.partial(write_out, groups),
        out_shape=jax.ShapeDtypeStruct((rows, channels), BF16),
        in_specs=[pl.BlockSpec(memory_space=pltpu.VMEM)] * 5,
        out_specs=pl.BlockSpec(memory_space=pltpu.HBM),
        scratch_shapes=[pltpu.VMEM((rows, LANES), BF16), pltpu.SemaphoreType.DMA((2,))],
        compiler_params=pltpu.CompilerParams(vmem_limit_bytes=4 * 1024 * 1024),
        name="write",
    )(*results)


def solution(mesh):
    axes = tuple(mesh.axis_names)
    placed = (P(axes, None), P(), P(), P(), P())
    return jax.shard_map(
        functools.partial(on_device, axes),
        mesh=mesh,
        in_specs=placed,
        out_specs=P(axes, None),
        check_vma=False,
    )
```

```python
import functools

import jax
import jax.numpy as jnp
from jax import lax
from jax.experimental import pallas as pl
from jax.experimental.pallas import tpu as pltpu
from jax.sharding import PartitionSpec as P

F32 = jnp.float32
BF16 = jnp.bfloat16
LANES = 128
CHUNKS = 16
EARLY = 5
MORE = 0
SIDE = 4
STEP = 4
LEAD = 16
NEAR = 9
SLICES = 16
HALVES = 2
MESH = pl.DeviceIdType.MESH


def lanes_of(c, width=LANES):
    return pl.ds(pl.multiple_of(c * width, width), width)


def row_scale(total, channels):
    mean = jnp.sum(total, axis=-1, keepdims=True) * (1.0 / channels)
    return jnp.broadcast_to(lax.rsqrt(mean + 1e-06), total.shape)


def square_sums(read, rows, blocks):
    def add(c, total):
        v = read(c).astype(F32)
        return total + v * v

    return lax.fori_loop(0, blocks, add, jnp.zeros((rows, LANES), F32))


def stream(z_ref, taps, first, rows):
    total = taps[0] * z_ref[8 + first : 8 + first + rows]
    for i in range(1, len(taps)):
        total = total + taps[i] * z_ref[8 + first - i : 8 + first - i + rows]
    return total


def feat_rows(feat_ref, o, gain, cs):
    streams, feat = feat_ref.shape[1:3]
    return [[feat_ref[0, j, i, o : o + 1, cs] * gain for i in range(feat)] for j in range(streams)]


def pieces(rows, most=48):
    return [(first, min(most, rows - first)) for first in range(0, rows, most)]


def short_block(c, read, rows, gain_ref, feat_ref, taps_ref, z_ref, w_ref, s_ref, h_ref, start, hs):
    cs = lanes_of(c)
    gain = gain_ref[0, 0:1, cs]
    taps = feat_rows(feat_ref, 0, gain, cs)
    short = [taps_ref[i, 0:1, cs] for i in range(taps_ref.shape[0])]
    z_ref[8 : 8 + rows] = read(c).astype(F32) * s_ref[:rows]
    for first, count in pieces(rows):
        u1 = stream(z_ref, taps[1], first, count)
        u2 = stream(z_ref, taps[2], first, count)
        w_ref[8 + first : 8 + first + count] = (u1 * u2).astype(BF16).astype(F32)
    for first, count in pieces(rows):
        f = stream(w_ref, short, first, count)
        u0 = stream(z_ref, taps[0], first, count)
        h_ref[start + first : start + first + count, hs] = u0 * f
    h = (h_ref[start : start + rows, hs] + read(c).astype(F32)).astype(BF16).astype(F32)
    h_ref[start : start + rows, hs] = h
    return h


def same_place(rows):
    return (lax.broadcasted_iota(jnp.int32, (rows, LANES), 0)
            == lax.broadcasted_iota(jnp.int32, (rows, LANES), 1))


def pack_rows(values_ref, start, rows, pack_ref):
    for r, (first, count) in enumerate(pieces(rows, LANES)):
        values = values_ref[start + first : start + first + count]
        pack_ref[r : r + 1] = jnp.sum(jnp.where(same_place(count), values, 0.0), axis=0, keepdims=True)


def unpack_rows(pack_ref, rows, values_ref):
    for r, (first, count) in enumerate(pieces(rows, LANES)):
        values = jnp.broadcast_to(pack_ref[r : r + 1], (count, LANES))
        column = jnp.sum(jnp.where(same_place(count), values, 0.0), axis=1, keepdims=True)
        values_ref[first : first + count] = jnp.broadcast_to(column, (count, LANES))


def combine(product, h, u, groups, half, write):
    lane_group = lax.broadcasted_iota(jnp.int32, (half, LANES), 1) // (LANES // groups)
    for side in range(2):
        ls = slice(side * LANES, (side + 1) * LANES)
        f = product[0:half, ls]
        for g in range(1, groups):
            f = jnp.where(lane_group == g, product[g * half : (g + 1) * half, ls], f)
        write(slice(side * half, (side + 1) * half), (h(side) + u(side) * f).astype(BF16))


def write_out(groups, main_ref, rhs_ref, table_ref, h_ref, u_ref, out_ref, end_ref, sems):
    rows, channels = main_ref.shape
    half = rows // 2
    width = channels - LANES
    main = pltpu.make_async_copy(main_ref.at[:, pl.ds(0, width)], out_ref.at[:, pl.ds(0, width)], sems.at[0])
    main.start()

    def write(rs, values):
        end_ref[rs] = values

    part = lambda ref: lambda side: ref[side * half : (side + 1) * half]
    product = jnp.dot(table_ref[...], rhs_ref[...], preferred_element_type=F32)
    combine(product, part(h_ref), part(u_ref), groups, half, write)
    end = pltpu.make_async_copy(end_ref, out_ref.at[:, pl.ds(width, LANES)], sems.at[1])
    end.start()
    main.wait()
    end.wait()


def kernel(axes, x_hbm, gain_hbm, feat_hbm, taps_hbm, mr_hbm, out_ref, end_rhs_ref, end_table_ref, end_h_ref, end_u_ref,
           x_ref, gain_ref, feat_ref, taps_ref, mr_ref,
           stage_ref, win_ref, h_ref, u_ref, table_ref, base_ref, rhs_ref, scale_ref, z_ref, w_ref,
           s_ref, sum_ref, halo_ref, behind_ref, told_ref, before_ref, give_ref, got_ref, near_ref, near_give_ref, near_got_ref, relay_ref,
           local_sems, lead_sems, send_sems, recv_sems, relay_send_sems, relay_recv_sems,
           side_ref, side_send_sems, side_recv_sems, last_send_sems, last_recv_sems, near_sems,
           first_give_ref, first_got_ref):
    rows, channels = x_ref.shape
    tap_count, group_count = mr_ref.shape[1:]
    per_group = channels // group_count
    groups = LANES // per_group
    half = rows // 2
    blocks = channels // LANES
    part = channels // CHUNKS
    here = blocks // CHUNKS
    tail = tap_count + LEAD
    first_tail = rows - tail
    first_sent = rows - tap_count
    side_start = EARLY + MORE
    side_end = side_start + SIDE
    near_width = channels // (SLICES * HALVES)
    far = LEAD - NEAR
    last_chunk = CHUNKS - 1
    outer, inner = axes
    inner_size = lax.axis_size(inner)
    count = lax.axis_size(outer) * inner_size
    me = lax.axis_index(outer) * inner_size + lax.axis_index(inner)
    behind, ahead = me - 1, me + 1
    has_behind, has_ahead = me > 0, me < count - 1
    sections, section = lax.axis_size(outer), lax.axis_index(outer)
    start_of, end_of = lax.axis_index(inner) == 0, lax.axis_index(inner) == inner_size - 1
    odd, even = section % 2 == 1, section % 2 == 0
    via_relay = end_of & odd & (section + 2 < sections)
    is_relay = end_of & odd & (section >= 3)
    is_side = start_of & even & (section + 3 < sections)
    past_relay = start_of & even & (section >= 2) & (section + 1 < sections)

    def place(index):
        return (index // inner_size, index % inner_size)

    barrier = pltpu.get_barrier_semaphore()

    @pl.when(has_behind)
    def _():
        pl.semaphore_signal(barrier, inc=1, device_id=place(behind), device_id_type=MESH)

    @pl.when(is_relay)
    def _():
        pl.semaphore_signal(barrier, inc=1, device_id=place(me - 2 * inner_size), device_id_type=MESH)

    @pl.when(is_side)
    def _():
        pl.semaphore_signal(barrier, inc=1, device_id=place(behind + 2 * inner_size), device_id_type=MESH)

    @pl.when(past_relay)
    def _():
        pl.semaphore_signal(barrier, inc=1, device_id=place(me - 2 * inner_size), device_id_type=MESH)
        pl.semaphore_signal(barrier, inc=1, device_id=place(behind + 2 * inner_size), device_id_type=MESH)

    loads = [pltpu.make_async_copy(src, dst, local_sems.at[i]) for i, (src, dst) in enumerate(
        [(x_hbm.at[pl.ds(rows - LEAD, LEAD)], x_ref.at[pl.ds(rows - LEAD, LEAD)]),
         (x_hbm.at[pl.ds(0, rows - LEAD)], x_ref.at[pl.ds(0, rows - LEAD)]), (gain_hbm, gain_ref), (feat_hbm, feat_ref), (taps_hbm, taps_ref), (mr_hbm, mr_ref)])]
    for load in loads:
        load.start()

    def to_device(index, src, dst, send_sem, recv_sem):
        return pltpu.make_async_remote_copy(
            src_ref=src, dst_ref=dst, send_sem=send_sem, recv_sem=recv_sem,
            device_id=place(index), device_id_type=MESH)

    to_ahead = functools.partial(to_device, ahead)

    def near_copy(p):
        return to_ahead(near_give_ref.at[p], near_got_ref.at[p], near_sems.at[0, p], near_sems.at[1, p])

    gives, gots = (first_give_ref, give_ref), (first_got_ref, got_ref)

    def tell_copy(o):
        return to_ahead(gives[o], gots[o], lead_sems.at[2 + 2 * o], lead_sems.at[3 + 2 * o])

    def part_copy(k):
        cs = lanes_of(k, part)
        return to_ahead(stage_ref.at[:, cs], win_ref.at[pl.ds(0, tap_count), cs],
                        send_sems.at[k], recv_sems.at[k])

    def to_relay_copy(k):
        cs = lanes_of(k, part)
        return to_device(me + 2 * inner_size, stage_ref.at[:, cs], relay_ref.at[:, cs], send_sems.at[k], relay_recv_sems.at[k])

    def from_relay_copy(k):
        cs = lanes_of(k, part)
        return to_device(me - 2 * inner_size + 1, relay_ref.at[:, cs], win_ref.at[pl.ds(0, tap_count), cs],
                         relay_send_sems.at[k], recv_sems.at[k])

    def side_columns(k):
        return lanes_of(k - side_start, part)

    def to_side_copy(k):
        return to_device(ahead - 2 * inner_size, stage_ref.at[:, lanes_of(k, part)],
                         side_ref.at[:, side_columns(k)], send_sems.at[k], side_recv_sems.at[k - side_start])

    def from_side_copy(k):
        return to_device(me + 2 * inner_size, side_ref.at[:, side_columns(k)],
                         win_ref.at[pl.ds(0, tap_count), lanes_of(k, part)],
                         side_send_sems.at[k - side_start], recv_sems.at[k])


    def last_copy(b):
        cs = lanes_of(last_chunk * here + b)
        return to_ahead(stage_ref.at[:, cs], win_ref.at[pl.ds(0, tap_count), cs],
                        last_send_sems.at[b], last_recv_sems.at[b])

    loads[0].wait()
    def near_columns(p, i):
        first = (p * SLICES + i) * near_width
        return slice(first, first + near_width)

    greeted = [has_ahead, via_relay, via_relay, is_relay, is_side]
    for p in range(HALVES):
        for i in range(SLICES):
            near_ref[i * NEAR : (i + 1) * NEAR] = x_ref[rows - LEAD :, near_columns(p, i)].astype(F32)[far:]
        near_give_ref[p] = near_ref[...].astype(BF16)
        if p == 0:
            pl.semaphore_wait(barrier, sum(g.astype(jnp.int32) for g in greeted))

        @pl.when(has_ahead)
        def _():
            near_copy(p).start()

    loads[1].wait()

    @pl.loop(0, EARLY)
    def _(k):
        @pl.loop(0, here)
        def _(b):
            cs = lanes_of(k * here + b)
            stage_ref[:, cs] = x_ref[first_tail:, cs].astype(F32)[far : far + tap_count].astype(BF16)

        @pl.when(has_ahead & jnp.logical_not(via_relay))
        def _():
            part_copy(k).start()

        @pl.when(via_relay)
        def _():
            to_relay_copy(k).start()

    z_ref[...] = jnp.zeros_like(z_ref)
    w_ref[...] = jnp.zeros_like(w_ref)
    give_ref[...] = jnp.zeros_like(give_ref)
    share = (gain_ref, feat_ref, taps_ref, z_ref, w_ref, s_ref)
    early_blocks = EARLY * here
    told_rows = len(pieces(tail, LANES))

    def mr_product(taps, first, size):
        return (stream(z_ref, taps[1], first, size) * stream(z_ref, taps[2], first, size)).astype(BF16)

    def with_first(row, product):
        first = lax.broadcasted_iota(jnp.int32, product.shape, 0) == 0
        return jnp.where(first, jnp.broadcast_to(row, product.shape), product.astype(F32)).astype(BF16)

    def mr_taps_of(cs):
        return feat_rows(feat_ref, 1, gain_ref[0, 1:2, cs], cs)

    read_tail = lambda c: x_ref[first_tail:, lanes_of(c)]
    s_ref[:tail] = row_scale(square_sums(read_tail, tail, blocks), channels)
    pack_rows(s_ref, 0, tail, first_give_ref)

    @pl.when(has_ahead)
    def _():
        tell_copy(0).start()

    for load in loads[2:]:
        load.wait()
    sum_ref[:tail] = jnp.zeros((tail, LANES), F32)
    start_tail = LEAD + first_tail

    @pl.loop(0, blocks)
    def _(c):
        h = short_block(c, read_tail, tail, *share, h_ref, start_tail, lanes_of(c))
        sum_ref[:tail] += h * h

    scale_ref[start_tail : start_tail + tail] = row_scale(sum_ref[:tail], channels)
    pack_rows(scale_ref, start_tail, tail, give_ref)
    for b in range(here):
        cs = slice((last_chunk * here + b) * LANES, (last_chunk * here + b + 1) * LANES)
        give_ref[told_rows + b : told_rows + b + 1] = h_ref[LEAD + rows - 2 : LEAD + rows - 1, cs]

    @pl.when(has_ahead)
    def _():
        tell_copy(1).start()

    def product_to_send(c):
        cs = lanes_of(c)
        taps = mr_taps_of(cs)
        n = tap_count + 8
        top = LEAD + first_sent - 8
        z_ref[0:n] = h_ref[top : top + n, cs] * scale_ref[top : top + n]
        for first, size in pieces(tap_count):
            product = mr_product(taps, first, size)
            win_ref[rows + first : rows + first + size, cs] = product
            if first == 0:
                product = with_first(h_ref[LEAD + rows - 2 : LEAD + rows - 1, cs], product)
            stage_ref[first : first + size, cs] = product

    @pl.loop(EARLY, last_chunk)
    def _(k):
        @pl.loop(0, here)
        def _(b):
            product_to_send(k * here + b)

        above = via_relay & (k < side_start)
        beside = via_relay & (k >= side_start) & (k < side_end)

        @pl.when(has_ahead & jnp.logical_not(above) & jnp.logical_not(beside))
        def _():
            part_copy(k).start()

        @pl.when(above)
        def _():
            to_relay_copy(k).start()

        @pl.when(beside)
        def _():
            to_side_copy(k).start()

    @pl.loop(0, here)
    def _(b):
        product_to_send(last_chunk * here + b)

        @pl.when(has_ahead)
        def _():
            last_copy(b).start()

    @pl.when(is_relay)
    def _():
        @pl.loop(0, EARLY)
        def _(k):
            to_relay_copy(k).wait_recv()
            from_relay_copy(k).start()

    at_tap = lax.broadcasted_iota(jnp.int32, (tap_count, tap_count), 0)
    at_lag = lax.broadcasted_iota(jnp.int32, (tap_count, tap_count), 1)
    flip = jnp.where((at_tap + at_lag == tap_count) | (at_tap + at_lag == 0), 1.0, 0.0).astype(BF16)
    past = (lax.broadcasted_iota(jnp.int32, (half, tap_count), 1)
            > lax.broadcasted_iota(jnp.int32, (half, tap_count), 0))
    base_ref[...] = lax.dot_general(mr_ref[0], flip, (((0,), (0,)), ((), ())),
                                    preferred_element_type=F32)
    rhs_ref[...] = jnp.zeros_like(rhs_ref)

    @pl.when(has_behind)
    def _():
        for p in range(HALVES):
            near_copy(p).wait_recv()

    @pl.when(jnp.logical_not(has_behind))
    def _():
        near_got_ref[...] = jnp.zeros_like(near_got_ref)
        got_ref[...] = jnp.zeros_like(got_ref)
        win_ref[:tap_count] = jnp.zeros((tap_count, channels), BF16)

    for p in range(HALVES):
        near_ref[...] = near_got_ref[p].astype(F32)
        for i in range(SLICES):
            cs = near_columns(p, i)
            before_ref[:far, cs] = jnp.zeros((far, near_width), F32)
            before_ref[far:, cs] = near_ref[i * NEAR : (i + 1) * NEAR]

    head = LEAD + first_sent
    z_ref[0:8] = jnp.zeros((8, LANES), F32)
    read_head = lambda c: jnp.concatenate(
        [before_ref[:, lanes_of(c)], x_ref[:first_sent, lanes_of(c)].astype(F32)], axis=0)
    s_ref[:head] = row_scale(square_sums(read_head, head, blocks), channels)
    sum_ref[:head] = jnp.zeros((head, LANES), F32)

    @pl.loop(0, blocks)
    def _(c):
        h = short_block(c, read_head, head, *share, h_ref, 0, lanes_of(c))
        sum_ref[:head] += h * h

    scale_ref[:head] = row_scale(sum_ref[:head], channels)

    @pl.loop(0, blocks)
    def _(c):
        cs = lanes_of(c)
        taps = mr_taps_of(cs)
        z_ref[0 : rows + 8] = h_ref[LEAD - 8 :, cs] * scale_ref[LEAD - 8 :]

        def put(low, high):
            for first, size in pieces(high - low):
                first += low
                win_ref[tap_count + first : tap_count + first + size, cs] = mr_product(taps, first, size)

        put(LEAD, first_sent)

        @pl.when(c < early_blocks)
        def _():
            put(first_sent, rows)

        for first, size in pieces(rows - LEAD):
            first += LEAD
            u_ref[first : first + size, cs] = stream(z_ref, taps[0], first, size)

    @pl.when(is_relay)
    def _():
        @pl.loop(EARLY, side_start)
        def _(k):
            to_relay_copy(k).wait_recv()
            from_relay_copy(k).start()

    @pl.when(is_side)
    def _():
        @pl.loop(side_start, side_end)
        def _(k):
            to_side_copy(k).wait_recv()
            from_side_copy(k).start()

    @pl.loop(0, blocks)
    def _(c):
        lags = base_ref[pl.ds(pl.multiple_of(c * groups, groups), groups), :]
        for g in range(groups):
            row = jnp.broadcast_to(lags[g : g + 1], (half, tap_count))
            turned = pltpu.roll(row, 0, 1, stride=1, stride_axis=0)
            gs = slice(g * half, (g + 1) * half)
            table_ref[c, gs, :tap_count] = jnp.where(past, turned, 0.0).astype(BF16)
            table_ref[c, gs, tap_count:] = jnp.where(past, 0.0, turned).astype(BF16)

    reach = half + tap_count

    @pl.when(has_behind)
    def _():
        tell_copy(0).wait_recv()
        unpack_rows(first_got_ref, tail, s_ref)
        tell_copy(1).wait_recv()
        unpack_rows(got_ref, tail, told_ref)
        scale_ref[LEAD - 2 : LEAD - 1] = told_ref[tail - 2 : tail - 1]

    behind_ref[:far] = jnp.zeros((far, LANES), F32)

    def first_rows(c, before):
        cs = lanes_of(c)
        taps = mr_taps_of(cs)
        h_ref[LEAD - 2 : LEAD - 1, cs] = before
        top = LEAD + 8
        z_ref[0:top] = h_ref[LEAD - 8 : LEAD + LEAD, cs] * scale_ref[LEAD - 8 : LEAD + LEAD]
        win_ref[tap_count : tap_count + LEAD, cs] = mr_product(taps, 0, LEAD)
        u_ref[0:LEAD, cs] = stream(z_ref, taps[0], 0, LEAD)

    shared = tap_count - half

    def place_own(c, slot):
        cs = lanes_of(c)
        rhs_ref[slot, tap_count:reach, :LANES] = win_ref[tap_count:reach, cs]
        rhs_ref[slot, shared:reach, LANES:] = win_ref[tap_count : half + reach, cs]

    def place_halo(c, slot):
        cs = lanes_of(c)
        rhs_ref[slot, :tap_count, :LANES] = win_ref[:tap_count, cs]
        rhs_ref[slot, :shared, LANES:] = win_ref[half:tap_count, cs]

    def finish(c, slot):
        cs = lanes_of(c)
        place_halo(c, slot)
        product = jnp.dot(table_ref[c], rhs_ref[slot], preferred_element_type=F32)

        def write(rs, values):
            out_ref[rs, cs] = values

        combine(product, lambda side: h_ref[LEAD + side * half : LEAD + (side + 1) * half, cs],
                lambda side: u_ref[side * half : (side + 1) * half, cs], groups, half, write)

    @pl.loop(0, last_chunk)
    def _(k):
        @pl.when(has_behind)
        def _():
            part_copy(k).wait_recv()

        @pl.when(has_behind & (k < EARLY))
        def _():
            @pl.loop(0, here)
            def _(b):
                c = k * here + b
                cs = lanes_of(c)
                behind_ref[far : far + tap_count] = win_ref[:tap_count, cs].astype(F32)
                behind_ref[far + tap_count :] = before_ref[far:, cs]
                short_block(c, lambda _: behind_ref[...], tail, *share, halo_ref, 0, slice(None))
                taps = mr_taps_of(cs)
                z_ref[0:tail] = halo_ref[...] * told_ref[...]
                for first, size in pieces(tap_count):
                    product = mr_product(taps, tail - tap_count - 8 + first, size)
                    if first == 0:
                        product = with_first(halo_ref[tail - 2 : tail - 1], product)
                    win_ref[first : first + size, cs] = product

        @pl.loop(0, here, step=STEP)
        def _(b):
            for slot in range(STEP):
                c = k * here + b + slot
                first_rows(c, win_ref[:LEAD, lanes_of(c)].astype(F32)[0:1])
            for slot in range(STEP):
                place_own(k * here + b + slot, slot)
                finish(k * here + b + slot, slot)

    for b in range(here):
        first_rows(last_chunk * here + b, got_ref[told_rows + b : told_rows + b + 1])
        place_own(last_chunk * here + b, b)

    end_rhs_ref[...] = rhs_ref[here - 1]
    end_table_ref[...] = table_ref[blocks - 1]
    end_h_ref[...] = h_ref[LEAD:, channels - LANES :]
    end_u_ref[...] = u_ref[:, channels - LANES :]

    @pl.loop(0, here - 1)
    def _(b):
        @pl.when(has_behind)
        def _():
            last_copy(b).wait_recv()

        finish(last_chunk * here + b, b)

    @pl.when(has_behind)
    def _():
        last_copy(here - 1).wait_recv()

    end_rhs_ref[:tap_count, :LANES] = win_ref[:tap_count, channels - LANES :]
    end_rhs_ref[:shared, LANES:] = win_ref[half:tap_count, channels - LANES :]

    @pl.when(has_ahead)
    def _():
        for p in range(HALVES):
            near_copy(p).wait_send()
        tell_copy(0).wait_send()
        tell_copy(1).wait_send()

        @pl.loop(0, last_chunk)
        def _(k):
            part_copy(k).wait_send()

        @pl.loop(0, here)
        def _(b):
            last_copy(b).wait_send()

    @pl.when(is_relay)
    def _():
        @pl.loop(0, side_start)
        def _(k):
            from_relay_copy(k).wait_send()

    @pl.when(is_side)
    def _():
        @pl.loop(side_start, side_end)
        def _(k):
            from_side_copy(k).wait_send()


def on_device(axes, tokens, norm_gain, feat_taps, se_taps, mr_taps):
    rows, channels = tokens.shape
    tap_count, group_count = mr_taps.shape[1:]
    groups = LANES * group_count // channels
    blocks = channels // LANES
    spread = 2 * tap_count
    here = blocks // CHUNKS
    near_width = channels // (SLICES * HALVES)
    operands = (tokens, norm_gain, feat_taps.transpose(0, 2, 3, 1, 4), se_taps.transpose(1, 0, 2), mr_taps)
    results = pl.pallas_call(
        functools.partial(kernel, axes),
        out_shape=(
            pltpu.VMEM((rows, channels), BF16),
            pltpu.VMEM((spread, 2 * LANES), BF16),
            pltpu.VMEM((groups * rows // 2, spread), BF16),
            pltpu.VMEM((rows, LANES), F32),
            pltpu.VMEM((rows, LANES), F32),
        ),
        in_specs=[pl.BlockSpec(memory_space=pltpu.HBM)] * 5,
        out_specs=(pl.BlockSpec(memory_space=pltpu.VMEM),) * 5,
        scratch_shapes=[pltpu.VMEM(a.shape, a.dtype) for a in operands] + [
            pltpu.VMEM((tap_count, channels), BF16),
            pltpu.VMEM((tap_count + rows, channels), BF16),
            pltpu.VMEM((LEAD + rows, channels), F32),
            pltpu.VMEM((rows, channels), F32),
            pltpu.VMEM((blocks, groups * rows // 2, spread), BF16),
            pltpu.VMEM((group_count, tap_count), F32),
            pltpu.VMEM((max(STEP, here), spread, 2 * LANES), BF16),
            pltpu.VMEM((LEAD + rows, LANES), F32),
            pltpu.VMEM((LEAD + rows, LANES), F32),
            pltpu.VMEM((LEAD + rows, LANES), F32),
            pltpu.VMEM((LEAD + rows, LANES), F32),
            pltpu.VMEM((LEAD + rows, LANES), F32),
            pltpu.VMEM((tap_count + LEAD, LANES), F32),
            pltpu.VMEM((tap_count + LEAD, LANES), F32),
            pltpu.VMEM((tap_count + LEAD, LANES), F32),
            pltpu.VMEM((LEAD, channels), F32),
            pltpu.VMEM((8, LANES), F32),
            pltpu.VMEM((8, LANES), F32),
            pltpu.VMEM((SLICES * NEAR, near_width), F32),
            pltpu.VMEM((HALVES, SLICES * NEAR, near_width), BF16),
            pltpu.VMEM((HALVES, SLICES * NEAR, near_width), BF16),
            pltpu.VMEM((tap_count, (EARLY + MORE) * channels // CHUNKS), BF16),
            pltpu.SemaphoreType.DMA((6,)),
            pltpu.SemaphoreType.DMA((6,)),
            pltpu.SemaphoreType.DMA((CHUNKS,)),
            pltpu.SemaphoreType.DMA((CHUNKS,)),
            pltpu.SemaphoreType.DMA((EARLY + MORE,)),
            pltpu.SemaphoreType.DMA((EARLY + MORE,)),
            pltpu.VMEM((tap_count, SIDE * channels // CHUNKS), BF16),
            pltpu.SemaphoreType.DMA((SIDE,)),
            pltpu.SemaphoreType.DMA((SIDE,)),
            pltpu.SemaphoreType.DMA((blocks // CHUNKS,)),
            pltpu.SemaphoreType.DMA((blocks // CHUNKS,)),
            pltpu.SemaphoreType.DMA((2, HALVES)),
            pltpu.VMEM((2, LANES), F32),
            pltpu.VMEM((2, LANES), F32),
        ],
        compiler_params=pltpu.CompilerParams(
            collective_id=0, has_side_effects=True, vmem_limit_bytes=57 * 1024 * 1024),
        name="pair",
    )(*operands)
    return pl.pallas_call(
        functools.partial(write_out, groups),
        out_shape=jax.ShapeDtypeStruct((rows, channels), BF16),
        in_specs=[pl.BlockSpec(memory_space=pltpu.VMEM)] * 5,
        out_specs=pl.BlockSpec(memory_space=pltpu.HBM),
        scratch_shapes=[pltpu.VMEM((rows, LANES), BF16), pltpu.SemaphoreType.DMA((2,))],
        compiler_params=pltpu.CompilerParams(vmem_limit_bytes=4 * 1024 * 1024),
        name="write",
    )(*results)


def solution(mesh):
    axes = tuple(mesh.axis_names)
    placed = (P(axes, None), P(), P(), P(), P())
    return jax.shard_map(
        functools.partial(on_device, axes),
        mesh=mesh,
        in_specs=placed,
        out_specs=P(axes, None),
        check_vma=False,
    )
```

```python
import functools

import jax
import jax.numpy as jnp
from jax import lax
from jax.experimental import pallas as pl
from jax.experimental.pallas import tpu as pltpu
from jax.sharding import PartitionSpec as P

F32 = jnp.float32
BF16 = jnp.bfloat16
LANES = 128
CHUNKS = 16
EARLY = 5
MORE = 0
SIDE = 4
STEP = 4
LEAD = 16
NEAR = 9
SLICES = 16
HALVES = 2
MESH = pl.DeviceIdType.MESH


def lanes_of(c, width=LANES):
    return pl.ds(pl.multiple_of(c * width, width), width)


def row_scale(total, channels):
    mean = jnp.sum(total, axis=-1, keepdims=True) * (1.0 / channels)
    return jnp.broadcast_to(lax.rsqrt(mean + 1e-06), total.shape)


def square_sums(read, rows, blocks):
    def add(c, total):
        v = read(c).astype(F32)
        return total + v * v

    return lax.fori_loop(0, blocks, add, jnp.zeros((rows, LANES), F32))


def stream(z_ref, taps, first, rows):
    total = taps[0] * z_ref[8 + first : 8 + first + rows]
    for i in range(1, len(taps)):
        total = total + taps[i] * z_ref[8 + first - i : 8 + first - i + rows]
    return total


def feat_rows(feat_ref, o, gain, cs):
    streams, feat = feat_ref.shape[1:3]
    return [[feat_ref[0, j, i, o : o + 1, cs] * gain for i in range(feat)] for j in range(streams)]


def pieces(rows, most=48):
    return [(first, min(most, rows - first)) for first in range(0, rows, most)]


def short_block(c, read, rows, gain_ref, feat_ref, taps_ref, z_ref, w_ref, s_ref, h_ref, start, hs):
    cs = lanes_of(c)
    gain = gain_ref[0, 0:1, cs]
    taps = feat_rows(feat_ref, 0, gain, cs)
    short = [taps_ref[i, 0:1, cs] for i in range(taps_ref.shape[0])]
    z_ref[8 : 8 + rows] = read(c).astype(F32) * s_ref[:rows]
    for first, count in pieces(rows):
        u1 = stream(z_ref, taps[1], first, count)
        u2 = stream(z_ref, taps[2], first, count)
        w_ref[8 + first : 8 + first + count] = (u1 * u2).astype(BF16).astype(F32)
    for first, count in pieces(rows):
        f = stream(w_ref, short, first, count)
        u0 = stream(z_ref, taps[0], first, count)
        h_ref[start + first : start + first + count, hs] = u0 * f
    h = (h_ref[start : start + rows, hs] + read(c).astype(F32)).astype(BF16).astype(F32)
    h_ref[start : start + rows, hs] = h
    return h


def same_place(rows):
    return (lax.broadcasted_iota(jnp.int32, (rows, LANES), 0)
            == lax.broadcasted_iota(jnp.int32, (rows, LANES), 1))


def pack_rows(values_ref, start, rows, pack_ref):
    for r, (first, count) in enumerate(pieces(rows, LANES)):
        values = values_ref[start + first : start + first + count]
        pack_ref[r : r + 1] = jnp.sum(jnp.where(same_place(count), values, 0.0), axis=0, keepdims=True)


def unpack_rows(pack_ref, rows, values_ref):
    for r, (first, count) in enumerate(pieces(rows, LANES)):
        values = jnp.broadcast_to(pack_ref[r : r + 1], (count, LANES))
        column = jnp.sum(jnp.where(same_place(count), values, 0.0), axis=1, keepdims=True)
        values_ref[first : first + count] = jnp.broadcast_to(column, (count, LANES))


def combine(product, h, u, groups, half, write):
    lane_group = lax.broadcasted_iota(jnp.int32, (half, LANES), 1) // (LANES // groups)
    for side in range(2):
        ls = slice(side * LANES, (side + 1) * LANES)
        f = product[0:half, ls]
        for g in range(1, groups):
            f = jnp.where(lane_group == g, product[g * half : (g + 1) * half, ls], f)
        write(slice(side * half, (side + 1) * half), (h(side) + u(side) * f).astype(BF16))


def write_out(groups, main_ref, rhs_ref, table_ref, h_ref, u_ref, out_ref, end_ref, sems):
    rows, channels = main_ref.shape
    half = rows // 2
    width = channels - LANES
    main = pltpu.make_async_copy(main_ref.at[:, pl.ds(0, width)], out_ref.at[:, pl.ds(0, width)], sems.at[0])
    main.start()

    def write(rs, values):
        end_ref[rs] = values

    part = lambda ref: lambda side: ref[side * half : (side + 1) * half]
    product = jnp.dot(table_ref[...], rhs_ref[...], preferred_element_type=F32)
    combine(product, part(h_ref), part(u_ref), groups, half, write)
    end = pltpu.make_async_copy(end_ref, out_ref.at[:, pl.ds(width, LANES)], sems.at[1])
    end.start()
    main.wait()
    end.wait()


def kernel(axes, x_hbm, gain_hbm, feat_hbm, taps_hbm, mr_hbm, out_ref, end_rhs_ref, end_table_ref, end_h_ref, end_u_ref,
           x_ref, gain_ref, feat_ref, taps_ref, mr_ref,
           stage_ref, win_ref, h_ref, u_ref, table_ref, base_ref, rhs_ref, scale_ref, z_ref, w_ref,
           s_ref, sum_ref, halo_ref, behind_ref, told_ref, before_ref, give_ref, got_ref, near_ref, near_give_ref, near_got_ref, relay_ref,
           local_sems, lead_sems, send_sems, recv_sems, relay_send_sems, relay_recv_sems,
           side_ref, side_send_sems, side_recv_sems, last_send_sems, last_recv_sems, near_sems,
           first_give_ref, first_got_ref):
    rows, channels = x_ref.shape
    tap_count, group_count = mr_ref.shape[1:]
    per_group = channels // group_count
    groups = LANES // per_group
    half = rows // 2
    blocks = channels // LANES
    part = channels // CHUNKS
    here = blocks // CHUNKS
    tail = tap_count + LEAD
    first_tail = rows - tail
    first_sent = rows - tap_count
    side_start = EARLY + MORE
    side_end = side_start + SIDE
    near_width = channels // (SLICES * HALVES)
    far = LEAD - NEAR
    last_chunk = CHUNKS - 1
    outer, inner = axes
    inner_size = lax.axis_size(inner)
    count = lax.axis_size(outer) * inner_size
    me = lax.axis_index(outer) * inner_size + lax.axis_index(inner)
    behind, ahead = me - 1, me + 1
    has_behind, has_ahead = me > 0, me < count - 1
    sections, section = lax.axis_size(outer), lax.axis_index(outer)
    start_of, end_of = lax.axis_index(inner) == 0, lax.axis_index(inner) == inner_size - 1
    odd, even = section % 2 == 1, section % 2 == 0
    via_relay = end_of & odd & (section + 2 < sections)
    is_relay = end_of & odd & (section >= 3)
    is_side = start_of & even & (section + 3 < sections)
    past_relay = start_of & even & (section >= 2) & (section + 1 < sections)

    def place(index):
        return (index // inner_size, index % inner_size)

    barrier = pltpu.get_barrier_semaphore()

    @pl.when(has_behind)
    def _():
        pl.semaphore_signal(barrier, inc=1, device_id=place(behind), device_id_type=MESH)

    @pl.when(is_relay)
    def _():
        pl.semaphore_signal(barrier, inc=1, device_id=place(me - 2 * inner_size), device_id_type=MESH)

    @pl.when(is_side)
    def _():
        pl.semaphore_signal(barrier, inc=1, device_id=place(behind + 2 * inner_size), device_id_type=MESH)

    @pl.when(past_relay)
    def _():
        pl.semaphore_signal(barrier, inc=1, device_id=place(me - 2 * inner_size), device_id_type=MESH)
        pl.semaphore_signal(barrier, inc=1, device_id=place(behind + 2 * inner_size), device_id_type=MESH)

    loads = [pltpu.make_async_copy(src, dst, local_sems.at[i]) for i, (src, dst) in enumerate(
        [(x_hbm.at[pl.ds(rows - LEAD, LEAD)], x_ref.at[pl.ds(rows - LEAD, LEAD)]),
         (x_hbm.at[pl.ds(0, rows - LEAD)], x_ref.at[pl.ds(0, rows - LEAD)]), (gain_hbm, gain_ref), (feat_hbm, feat_ref), (taps_hbm, taps_ref), (mr_hbm, mr_ref)])]
    for load in loads:
        load.start()

    def to_device(index, src, dst, send_sem, recv_sem):
        return pltpu.make_async_remote_copy(
            src_ref=src, dst_ref=dst, send_sem=send_sem, recv_sem=recv_sem,
            device_id=place(index), device_id_type=MESH)

    to_ahead = functools.partial(to_device, ahead)

    def near_copy(p):
        return to_ahead(near_give_ref.at[p], near_got_ref.at[p], near_sems.at[0, p], near_sems.at[1, p])

    gives, gots = (first_give_ref, give_ref), (first_got_ref, got_ref)

    def tell_copy(o):
        return to_ahead(gives[o], gots[o], lead_sems.at[2 + 2 * o], lead_sems.at[3 + 2 * o])

    def part_copy(k):
        cs = lanes_of(k, part)
        return to_ahead(stage_ref.at[:, cs], win_ref.at[pl.ds(0, tap_count), cs],
                        send_sems.at[k], recv_sems.at[k])

    def to_relay_copy(k):
        cs = lanes_of(k, part)
        return to_device(me + 2 * inner_size, stage_ref.at[:, cs], relay_ref.at[:, cs], send_sems.at[k], relay_recv_sems.at[k])

    def from_relay_copy(k):
        cs = lanes_of(k, part)
        return to_device(me - 2 * inner_size + 1, relay_ref.at[:, cs], win_ref.at[pl.ds(0, tap_count), cs],
                         relay_send_sems.at[k], recv_sems.at[k])

    def side_columns(k):
        return lanes_of(k - side_start, part)

    def to_side_copy(k):
        return to_device(ahead - 2 * inner_size, stage_ref.at[:, lanes_of(k, part)],
                         side_ref.at[:, side_columns(k)], send_sems.at[k], side_recv_sems.at[k - side_start])

    def from_side_copy(k):
        return to_device(me + 2 * inner_size, side_ref.at[:, side_columns(k)],
                         win_ref.at[pl.ds(0, tap_count), lanes_of(k, part)],
                         side_send_sems.at[k - side_start], recv_sems.at[k])


    def last_copy(b):
        cs = lanes_of(last_chunk * here + b)
        return to_ahead(stage_ref.at[:, cs], win_ref.at[pl.ds(0, tap_count), cs],
                        last_send_sems.at[b], last_recv_sems.at[b])

    loads[0].wait()
    def near_columns(p, i):
        first = (p * SLICES + i) * near_width
        return slice(first, first + near_width)

    greeted = [has_ahead, via_relay, via_relay, is_relay, is_side]
    for p in range(HALVES):
        for i in range(SLICES):
            near_ref[i * NEAR : (i + 1) * NEAR] = x_ref[rows - LEAD :, near_columns(p, i)].astype(F32)[far:]
        near_give_ref[p] = near_ref[...].astype(BF16)
        if p == 0:
            pl.semaphore_wait(barrier, sum(g.astype(jnp.int32) for g in greeted))

        @pl.when(has_ahead)
        def _():
            near_copy(p).start()

    loads[1].wait()

    @pl.loop(0, EARLY)
    def _(k):
        @pl.loop(0, here)
        def _(b):
            cs = lanes_of(k * here + b)
            stage_ref[:, cs] = x_ref[first_tail:, cs].astype(F32)[far : far + tap_count].astype(BF16)

        @pl.when(has_ahead & jnp.logical_not(via_relay))
        def _():
            part_copy(k).start()

        @pl.when(via_relay)
        def _():
            to_relay_copy(k).start()

    z_ref[...] = jnp.zeros_like(z_ref)
    w_ref[...] = jnp.zeros_like(w_ref)
    give_ref[...] = jnp.zeros_like(give_ref)
    share = (gain_ref, feat_ref, taps_ref, z_ref, w_ref, s_ref)
    early_blocks = EARLY * here
    told_rows = len(pieces(tail, LANES))

    def mr_product(taps, first, size):
        return (stream(z_ref, taps[1], first, size) * stream(z_ref, taps[2], first, size)).astype(BF16)

    def with_first(row, product):
        first = lax.broadcasted_iota(jnp.int32, product.shape, 0) == 0
        return jnp.where(first, jnp.broadcast_to(row, product.shape), product.astype(F32)).astype(BF16)

    def mr_taps_of(cs):
        return feat_rows(feat_ref, 1, gain_ref[0, 1:2, cs], cs)

    read_tail = lambda c: x_ref[first_tail:, lanes_of(c)]
    s_ref[:tail] = row_scale(square_sums(read_tail, tail, blocks), channels)
    pack_rows(s_ref, 0, tail, first_give_ref)

    @pl.when(has_ahead)
    def _():
        tell_copy(0).start()

    for load in loads[2:]:
        load.wait()
    sum_ref[:tail] = jnp.zeros((tail, LANES), F32)
    start_tail = LEAD + first_tail

    @pl.loop(0, blocks)
    def _(c):
        h = short_block(c, read_tail, tail, *share, h_ref, start_tail, lanes_of(c))
        sum_ref[:tail] += h * h

    scale_ref[start_tail : start_tail + tail] = row_scale(sum_ref[:tail], channels)
    pack_rows(scale_ref, start_tail, tail, give_ref)
    for b in range(here):
        cs = slice((last_chunk * here + b) * LANES, (last_chunk * here + b + 1) * LANES)
        give_ref[told_rows + b : told_rows + b + 1] = h_ref[LEAD + rows - 2 : LEAD + rows - 1, cs]

    @pl.when(has_ahead)
    def _():
        tell_copy(1).start()

    def product_to_send(c):
        cs = lanes_of(c)
        taps = mr_taps_of(cs)
        n = tap_count + 8
        top = LEAD + first_sent - 8
        z_ref[0:n] = h_ref[top : top + n, cs] * scale_ref[top : top + n]
        for first, size in pieces(tap_count):
            product = mr_product(taps, first, size)
            win_ref[rows + first : rows + first + size, cs] = product
            if first == 0:
                product = with_first(h_ref[LEAD + rows - 2 : LEAD + rows - 1, cs], product)
            stage_ref[first : first + size, cs] = product

    @pl.loop(EARLY, last_chunk)
    def _(k):
        @pl.loop(0, here)
        def _(b):
            product_to_send(k * here + b)

        above = via_relay & (k < side_start)
        beside = via_relay & (k >= side_start) & (k < side_end)

        @pl.when(has_ahead & jnp.logical_not(above) & jnp.logical_not(beside))
        def _():
            part_copy(k).start()

        @pl.when(above)
        def _():
            to_relay_copy(k).start()

        @pl.when(beside)
        def _():
            to_side_copy(k).start()

    @pl.loop(0, here)
    def _(b):
        product_to_send(last_chunk * here + b)

        @pl.when(has_ahead)
        def _():
            last_copy(b).start()

    @pl.when(is_relay)
    def _():
        @pl.loop(0, EARLY)
        def _(k):
            to_relay_copy(k).wait_recv()
            from_relay_copy(k).start()

    at_tap = lax.broadcasted_iota(jnp.int32, (tap_count, tap_count), 0)
    at_lag = lax.broadcasted_iota(jnp.int32, (tap_count, tap_count), 1)
    flip = jnp.where((at_tap + at_lag == tap_count) | (at_tap + at_lag == 0), 1.0, 0.0).astype(BF16)
    past = (lax.broadcasted_iota(jnp.int32, (half, tap_count), 1)
            > lax.broadcasted_iota(jnp.int32, (half, tap_count), 0))
    base_ref[...] = lax.dot_general(mr_ref[0], flip, (((0,), (0,)), ((), ())),
                                    preferred_element_type=F32)
    rhs_ref[...] = jnp.zeros_like(rhs_ref)

    @pl.when(has_behind)
    def _():
        for p in range(HALVES):
            near_copy(p).wait_recv()

    @pl.when(jnp.logical_not(has_behind))
    def _():
        near_got_ref[...] = jnp.zeros_like(near_got_ref)
        got_ref[...] = jnp.zeros_like(got_ref)
        win_ref[:tap_count] = jnp.zeros((tap_count, channels), BF16)

    for p in range(HALVES):
        near_ref[...] = near_got_ref[p].astype(F32)
        for i in range(SLICES):
            cs = near_columns(p, i)
            before_ref[:far, cs] = jnp.zeros((far, near_width), F32)
            before_ref[far:, cs] = near_ref[i * NEAR : (i + 1) * NEAR]

    head = LEAD + first_sent
    z_ref[0:8] = jnp.zeros((8, LANES), F32)
    read_head = lambda c: jnp.concatenate(
        [before_ref[:, lanes_of(c)], x_ref[:first_sent, lanes_of(c)].astype(F32)], axis=0)
    s_ref[:head] = row_scale(square_sums(read_head, head, blocks), channels)
    sum_ref[:head] = jnp.zeros((head, LANES), F32)

    @pl.loop(0, blocks)
    def _(c):
        h = short_block(c, read_head, head, *share, h_ref, 0, lanes_of(c))
        sum_ref[:head] += h * h

    scale_ref[:head] = row_scale(sum_ref[:head], channels)

    @pl.loop(0, blocks)
    def _(c):
        cs = lanes_of(c)
        taps = mr_taps_of(cs)
        z_ref[0 : rows + 8] = h_ref[LEAD - 8 :, cs] * scale_ref[LEAD - 8 :]

        def put(low, high):
            for first, size in pieces(high - low):
                first += low
                win_ref[tap_count + first : tap_count + first + size, cs] = mr_product(taps, first, size)

        put(LEAD, first_sent)

        @pl.when(c < early_blocks)
        def _():
            put(first_sent, rows)

        for first, size in pieces(rows - LEAD):
            first += LEAD
            u_ref[first : first + size, cs] = stream(z_ref, taps[0], first, size)

    @pl.when(is_relay)
    def _():
        @pl.loop(EARLY, side_start)
        def _(k):
            to_relay_copy(k).wait_recv()
            from_relay_copy(k).start()

    @pl.when(is_side)
    def _():
        @pl.loop(side_start, side_end)
        def _(k):
            to_side_copy(k).wait_recv()
            from_side_copy(k).start()

    @pl.loop(0, blocks)
    def _(c):
        lags = base_ref[pl.ds(pl.multiple_of(c * groups, groups), groups), :]
        for g in range(groups):
            row = jnp.broadcast_to(lags[g : g + 1], (half, tap_count))
            turned = pltpu.roll(row, 0, 1, stride=1, stride_axis=0)
            gs = slice(g * half, (g + 1) * half)
            table_ref[c, gs, :tap_count] = jnp.where(past, turned, 0.0).astype(BF16)
            table_ref[c, gs, tap_count:] = jnp.where(past, 0.0, turned).astype(BF16)

    reach = half + tap_count

    @pl.when(has_behind)
    def _():
        tell_copy(0).wait_recv()
        unpack_rows(first_got_ref, tail, s_ref)
        tell_copy(1).wait_recv()
        unpack_rows(got_ref, tail, told_ref)
        scale_ref[LEAD - 2 : LEAD - 1] = told_ref[tail - 2 : tail - 1]

    behind_ref[:far] = jnp.zeros((far, LANES), F32)

    def first_rows(c, before):
        cs = lanes_of(c)
        taps = mr_taps_of(cs)
        h_ref[LEAD - 2 : LEAD - 1, cs] = before
        top = LEAD + 8
        z_ref[0:top] = h_ref[LEAD - 8 : LEAD + LEAD, cs] * scale_ref[LEAD - 8 : LEAD + LEAD]
        win_ref[tap_count : tap_count + LEAD, cs] = mr_product(taps, 0, LEAD)
        u_ref[0:LEAD, cs] = stream(z_ref, taps[0], 0, LEAD)

    shared = tap_count - half

    def place_own(c, slot):
        cs = lanes_of(c)
        rhs_ref[slot, tap_count:reach, :LANES] = win_ref[tap_count:reach, cs]
        rhs_ref[slot, shared:reach, LANES:] = win_ref[tap_count : half + reach, cs]

    def place_halo(c, slot):
        cs = lanes_of(c)
        rhs_ref[slot, :tap_count, :LANES] = win_ref[:tap_count, cs]
        rhs_ref[slot, :shared, LANES:] = win_ref[half:tap_count, cs]

    def finish(c, slot):
        cs = lanes_of(c)
        place_halo(c, slot)
        product = jnp.dot(table_ref[c], rhs_ref[slot], preferred_element_type=F32)

        def write(rs, values):
            out_ref[rs, cs] = values

        combine(product, lambda side: h_ref[LEAD + side * half : LEAD + (side + 1) * half, cs],
                lambda side: u_ref[side * half : (side + 1) * half, cs], groups, half, write)

    @pl.loop(0, last_chunk)
    def _(k):
        @pl.when(has_behind)
        def _():
            part_copy(k).wait_recv()

        @pl.when(has_behind & (k < EARLY))
        def _():
            @pl.loop(0, here)
            def _(b):
                c = k * here + b
                cs = lanes_of(c)
                behind_ref[far : far + tap_count] = win_ref[:tap_count, cs].astype(F32)
                behind_ref[far + tap_count :] = before_ref[far:, cs]
                short_block(c, lambda _: behind_ref[...], tail, *share, halo_ref, 0, slice(None))
                taps = mr_taps_of(cs)
                z_ref[0:tail] = halo_ref[...] * told_ref[...]
                for first, size in pieces(tap_count):
                    product = mr_product(taps, tail - tap_count - 8 + first, size)
                    if first == 0:
                        product = with_first(halo_ref[tail - 2 : tail - 1], product)
                    win_ref[first : first + size, cs] = product

        @pl.loop(0, here, step=STEP)
        def _(b):
            for slot in range(STEP):
                c = k * here + b + slot
                first_rows(c, win_ref[:LEAD, lanes_of(c)].astype(F32)[0:1])
            for slot in range(STEP):
                place_own(k * here + b + slot, slot)
                finish(k * here + b + slot, slot)

    for b in range(here):
        first_rows(last_chunk * here + b, got_ref[told_rows + b : told_rows + b + 1])
        place_own(last_chunk * here + b, b)

    end_rhs_ref[...] = rhs_ref[here - 1]
    end_table_ref[...] = table_ref[blocks - 1]
    end_h_ref[...] = h_ref[LEAD:, channels - LANES :]
    end_u_ref[...] = u_ref[:, channels - LANES :]

    @pl.loop(0, here - 1)
    def _(b):
        @pl.when(has_behind)
        def _():
            last_copy(b).wait_recv()

        finish(last_chunk * here + b, b)

    @pl.when(has_ahead)
    def _():
        for p in range(HALVES):
            near_copy(p).wait_send()
        tell_copy(0).wait_send()
        tell_copy(1).wait_send()

        @pl.loop(0, last_chunk)
        def _(k):
            part_copy(k).wait_send()

        @pl.loop(0, here - 1)
        def _(b):
            last_copy(b).wait_send()

    @pl.when(is_relay)
    def _():
        @pl.loop(0, side_start)
        def _(k):
            from_relay_copy(k).wait_send()

    @pl.when(is_side)
    def _():
        @pl.loop(side_start, side_end)
        def _(k):
            from_side_copy(k).wait_send()

    @pl.when(has_behind)
    def _():
        last_copy(here - 1).wait_recv()

    end_rhs_ref[:tap_count, :LANES] = win_ref[:tap_count, channels - LANES :]
    end_rhs_ref[:shared, LANES:] = win_ref[half:tap_count, channels - LANES :]

    @pl.when(has_ahead)
    def _():
        last_copy(here - 1).wait_send()


def on_device(axes, tokens, norm_gain, feat_taps, se_taps, mr_taps):
    rows, channels = tokens.shape
    tap_count, group_count = mr_taps.shape[1:]
    groups = LANES * group_count // channels
    blocks = channels // LANES
    spread = 2 * tap_count
    here = blocks // CHUNKS
    near_width = channels // (SLICES * HALVES)
    operands = (tokens, norm_gain, feat_taps.transpose(0, 2, 3, 1, 4), se_taps.transpose(1, 0, 2), mr_taps)
    results = pl.pallas_call(
        functools.partial(kernel, axes),
        out_shape=(
            pltpu.VMEM((rows, channels), BF16),
            pltpu.VMEM((spread, 2 * LANES), BF16),
            pltpu.VMEM((groups * rows // 2, spread), BF16),
            pltpu.VMEM((rows, LANES), F32),
            pltpu.VMEM((rows, LANES), F32),
        ),
        in_specs=[pl.BlockSpec(memory_space=pltpu.HBM)] * 5,
        out_specs=(pl.BlockSpec(memory_space=pltpu.VMEM),) * 5,
        scratch_shapes=[pltpu.VMEM(a.shape, a.dtype) for a in operands] + [
            pltpu.VMEM((tap_count, channels), BF16),
            pltpu.VMEM((tap_count + rows, channels), BF16),
            pltpu.VMEM((LEAD + rows, channels), F32),
            pltpu.VMEM((rows, channels), F32),
            pltpu.VMEM((blocks, groups * rows // 2, spread), BF16),
            pltpu.VMEM((group_count, tap_count), F32),
            pltpu.VMEM((max(STEP, here), spread, 2 * LANES), BF16),
            pltpu.VMEM((LEAD + rows, LANES), F32),
            pltpu.VMEM((LEAD + rows, LANES), F32),
            pltpu.VMEM((LEAD + rows, LANES), F32),
            pltpu.VMEM((LEAD + rows, LANES), F32),
            pltpu.VMEM((LEAD + rows, LANES), F32),
            pltpu.VMEM((tap_count + LEAD, LANES), F32),
            pltpu.VMEM((tap_count + LEAD, LANES), F32),
            pltpu.VMEM((tap_count + LEAD, LANES), F32),
            pltpu.VMEM((LEAD, channels), F32),
            pltpu.VMEM((8, LANES), F32),
            pltpu.VMEM((8, LANES), F32),
            pltpu.VMEM((SLICES * NEAR, near_width), F32),
            pltpu.VMEM((HALVES, SLICES * NEAR, near_width), BF16),
            pltpu.VMEM((HALVES, SLICES * NEAR, near_width), BF16),
            pltpu.VMEM((tap_count, (EARLY + MORE) * channels // CHUNKS), BF16),
            pltpu.SemaphoreType.DMA((6,)),
            pltpu.SemaphoreType.DMA((6,)),
            pltpu.SemaphoreType.DMA((CHUNKS,)),
            pltpu.SemaphoreType.DMA((CHUNKS,)),
            pltpu.SemaphoreType.DMA((EARLY + MORE,)),
            pltpu.SemaphoreType.DMA((EARLY + MORE,)),
            pltpu.VMEM((tap_count, SIDE * channels // CHUNKS), BF16),
            pltpu.SemaphoreType.DMA((SIDE,)),
            pltpu.SemaphoreType.DMA((SIDE,)),
            pltpu.SemaphoreType.DMA((blocks // CHUNKS,)),
            pltpu.SemaphoreType.DMA((blocks // CHUNKS,)),
            pltpu.SemaphoreType.DMA((2, HALVES)),
            pltpu.VMEM((2, LANES), F32),
            pltpu.VMEM((2, LANES), F32),
        ],
        compiler_params=pltpu.CompilerParams(
            collective_id=0, has_side_effects=True, vmem_limit_bytes=57 * 1024 * 1024),
        name="pair",
    )(*operands)
    return pl.pallas_call(
        functools.partial(write_out, groups),
        out_shape=jax.ShapeDtypeStruct((rows, channels), BF16),
        in_specs=[pl.BlockSpec(memory_space=pltpu.VMEM)] * 5,
        out_specs=pl.BlockSpec(memory_space=pltpu.HBM),
        scratch_shapes=[pltpu.VMEM((rows, LANES), BF16), pltpu.SemaphoreType.DMA((2,))],
        compiler_params=pltpu.CompilerParams(vmem_limit_bytes=4 * 1024 * 1024),
        name="write",
    )(*results)


def solution(mesh):
    axes = tuple(mesh.axis_names)
    placed = (P(axes, None), P(), P(), P(), P())
    return jax.shard_map(
        functools.partial(on_device, axes),
        mesh=mesh,
        in_specs=placed,
        out_specs=P(axes, None),
        check_vma=False,
    )
```
